256 devices in a mesh: grp: 8 (over x_hi, y), tile: 32 (over x_lo, z, core).
Axes of the slice: x: 4 (x_hi: 2, x_lo: 2; x = x_hi * 2 + x_lo), y: 4, z: 8, core: 2. Of those that a mesh axis runs over, the one named last changes fastest.
Arguments:
- tracers: float32 [64, 9, 768, 128], P('grp', None, 'tile'), may hold values from -6 to 6
- wind_x: float32 [2, 9, 32, 24, 128], P(None, None, 'tile', 'grp'), may hold values from -0.5 to 0.5, as said below
- wind_y: float32 [2, 9, 32, 24, 128], P(None, None, 'tile', 'grp'), may hold values from -0.1 to 0.1
- surface_p: float32 [2, 32, 24, 128], P(None, 'tile', 'grp'), may hold values from 0.8 to 1.2
- coef_a: float32 [9], replicated, may hold values from 0.8 to 1.2
- coef_b: float32 [9], replicated, may hold values from 0.3 to 0.7
- edge_flip: int32 [32], replicated, may hold values from 0 to 1
Outputs:
- tracers_out: float32 [64, 9, 768, 128], P('grp', None, 'tile')
- air_mass: float32 [9, 768, 128], P(None, 'tile')
The draws below stay inside these ranges and needn't reach their ends.
Inputs may be any that keep to these rules, and one draw needn't show every extreme that they name: `edge_flip`: one entry for each edge of the cycle of tiles. `wind_x`: within each step and level all entries have the same sign, and their magnitudes lie between 0.25 and 0.5.
All inputs are finite; a program needn't handle non-finite values.
Results may differ from the reference program's by a relative error of at most 0.0003.
Values sent between devices are 32-bit elements; how exact they have to be, the bound alone decides.
No kernel may reach another device: no remote copies, remote signals or barrier semaphores. Data moves between devices by JAX's collectives and lax.ppermute only.
A program may use at most 64 MiB of HBM per device.

```python
import jax
import jax.numpy as jnp
from jax import lax

LEV = 9
STEPS = 2
CX = 24
NY = 128
TILES = 32
NX = 768
TRACERS = 64


def draw_wind_x(key, part):
    sign_key = jax.random.fold_in(key, 11)
    size_key = jax.random.fold_in(key, 12)
    sign_bits = jax.random.randint(sign_key, (STEPS, LEV, 1, 1, 1), 0, 2)
    sign_field = (2 * sign_bits - 1).astype(jnp.float32)
    fraction = jax.random.uniform(size_key, (STEPS, LEV, TILES, CX, NY), jnp.float32)
    magnitude = 0.25 + 0.25 * fraction
    return (sign_field * magnitude).astype(jnp.float32)


def touch_ends(drawn, stream_key, smallest, top_value):
    dims = drawn.shape
    index_at = [jax.random.randint(jax.random.fold_in(stream_key, axis), (), 0, dims[axis]) for axis in range(len(dims))]
    drawn = drawn.at[tuple(index_at)].set(smallest)
    longest = dims.index(max(dims))
    index_at[longest] = (index_at[longest] + 1) % dims[longest]
    return drawn.at[tuple(index_at)].set(top_value)


def level_of(own_key, extent, cuts, smallest, top_value):
    def one(dim, blocks):
        draws = jax.random.uniform(jax.random.fold_in(jax.random.fold_in(own_key, 6), dim), (blocks,), jnp.float32, smallest / len(cuts), top_value / len(cuts))
        return jnp.repeat(jnp.exp(draws), extent[dim] // blocks).reshape((-1,) + (1,) * (len(extent) - dim - 1))

    level = one(*cuts[0])
    for cut in cuts[1:]:
        level = level * one(*cut)
    return level


def normal_values(own_key, extent, scale, most, cuts=(), held_as=jnp.bfloat16):
    entries = jax.random.normal(own_key, extent, jnp.float32) * scale
    if len(cuts) > 0:
        entries = level_of(own_key, extent, cuts, -0.22, 0.18) * entries
    return jnp.clip(entries, min=-most, max=most).astype(held_as)


def setup_inputs(seed: int = 0) -> dict:
    keys = jax.random.split(jax.random.key(seed), 8)
    return {
        "tracers": normal_values(keys[0], (TRACERS, LEV, NX, NY), 1.0, 6.0, ((0, 8), (2, 32)), jnp.float32),
        "wind_x": draw_wind_x(jax.random.fold_in(keys[7], 71), 0),
        "wind_y": jnp.clip(jax.random.uniform(keys[2], (STEPS, LEV, TILES, CX, NY), jnp.float32, -0.1, 0.1) * level_of(keys[2], (STEPS, LEV, TILES, CX, NY), ((2, 32), (3, 8)), -0.4, 0.0), -0.1, 0.1),
        "surface_p": jnp.clip(0.8 + 0.40000004 * jax.random.uniform(keys[3], (STEPS, TILES, CX, NY), jnp.float32) ** level_of(keys[3], (STEPS, TILES, CX, NY), ((1, 32), (2, 8)), -0.2, 0.2), 0.8, 1.2),
        "coef_a": jnp.clip(jax.random.uniform(keys[4], (LEV,), jnp.float32, 0.8, 1.2), 0.8, 1.2),
        "coef_b": jnp.clip(jax.random.uniform(keys[5], (LEV,), jnp.float32, 0.3, 0.7), 0.3, 0.7),
        "edge_flip": touch_ends(jax.random.randint(keys[6], (TILES,), 0, 2), jax.random.fold_in(keys[6], 1), 0, 1).astype(jnp.int32),
    }


SECTION_WEIGHTS = (1.0 / 3.0, 0.5, 1.0)


def face_values(extended, faces, flux, axis):
    def cut(offset):
        return lax.slice_in_dim(extended, offset, offset + faces, axis=axis)
    plus = (2.0 * cut(0) - 13.0 * cut(1) + 47.0 * cut(2) + 27.0 * cut(3) - 3.0 * cut(4)) / 60.0
    minus = (2.0 * cut(5) - 13.0 * cut(4) + 47.0 * cut(3) + 27.0 * cut(2) - 3.0 * cut(1)) / 60.0
    return flux * jnp.where(flux >= 0.0, plus, minus)


def pad_second(values):
    lower = jnp.repeat(values[..., :1], 3, axis=-1)
    upper = jnp.repeat(values[..., -1:], 3, axis=-1)
    return jnp.concatenate([lower, values, upper], axis=-1)


def x_faces(flux):
    return 0.5 * (flux[..., :-1, :] + flux[..., 1:, :])


def y_faces(flux):
    inner = 0.5 * (flux[..., :-1] + flux[..., 1:])
    zeros = jnp.zeros(inner.shape[:-1] + (1,), jnp.float32)
    return jnp.concatenate([zeros, inner, zeros], axis=-1)


def divergence(along_x, along_y):
    return (along_x[..., 1:, :] - along_x[..., :-1, :]) + (along_y[..., 1:] - along_y[..., :-1])


def section(extended, face_x, face_y, div_mass, start_tracer, start_mass, weight):
    count = face_x.shape[-2] - 1
    width_y = extended.shape[-1]
    middle = lax.slice_in_dim(extended, 3, 3 + count, axis=extended.ndim - 2)
    along_x = face_values(extended, count + 1, face_x, extended.ndim - 2)
    along_y = face_values(pad_second(middle), width_y + 1, face_y, extended.ndim - 1)
    tracer_mass = start_tracer - weight * divergence(along_x, along_y)
    mass = start_mass - weight * div_mass
    return tracer_mass / mass, mass


def cycle_extend(field, width, edge_flip):
    tile_axis = field.ndim - 3
    left_source = jnp.roll(field, 1, axis=tile_axis)[..., -width:, :]
    right_source = jnp.roll(field, -1, axis=tile_axis)[..., :width, :]
    left_flag = (jnp.roll(edge_flip, 1) == 1)[:, None, None]
    right_flag = (edge_flip == 1)[:, None, None]
    left = jnp.where(left_flag, left_source[..., ::-1], left_source)
    right = jnp.where(right_flag, right_source[..., ::-1], right_source)
    return jnp.concatenate([left, field, right], axis=field.ndim - 2)


def reference(tracers, wind_x, wind_y, surface_p, coef_a, coef_b, edge_flip):
    met_mass = coef_a[None, :, None, None, None] + coef_b[None, :, None, None, None] * surface_p[:, None]
    flux_x = wind_x * met_mass
    flux_y = wind_y * met_mass
    faces_first = []
    faces_second = []
    divs = []
    start_masses = []
    mass = met_mass[0]
    for step_index in range(STEPS):
        face_x = x_faces(cycle_extend(flux_x[step_index], 1, edge_flip))
        face_y = y_faces(flux_y[step_index])
        div_mass = divergence(face_x, face_y)
        faces_first.append(face_x)
        faces_second.append(face_y)
        divs.append(div_mass)
        start_masses.append(mass)
        mass = mass - 1.0 * div_mass

    def advect(tracer):
        field = tracer.reshape(LEV, TILES, CX, NY)
        for step_index in range(STEPS):
            start_mass = start_masses[step_index]
            start_tracer = field * start_mass
            current = field
            for weight in SECTION_WEIGHTS:
                extended = cycle_extend(current, 3, edge_flip)
                current, unused = section(extended, faces_first[step_index], faces_second[step_index],
                                        divs[step_index], start_tracer, start_mass, weight)
            field = current
        return field.reshape(LEV, NX, NY)

    advected = lax.map(advect, tracers)
    return advected, mass.reshape(LEV, NX, NY)
```

```python
import functools

import jax
import jax.numpy as jnp
from jax import lax
from jax.experimental import pallas as pl
from jax.experimental.pallas import tpu as pltpu
from jax.sharding import PartitionSpec as P

SECTION_WEIGHTS = (1.0 / 3.0, 0.5, 1.0)
VMEM_LIMIT = 48 * 1024 * 1024


def ring(count, step):
    return [(i, (i + step) % count) for i in range(count)]


def advect_kernel(
    dims,
    sign_ref,
    flip_ref,
    gain_a_ref,
    gain_b_ref,
    own_ref,
    low_ref,
    high_ref,
    met_own_ref,
    met_low_ref,
    met_high_ref,
    out_ref,
    mass_ref,
    q_a,
    q_b,
    q_c,
    start_ref,
    flux_x_ref,
    band_ref,
    inverse_ref,
    mass_row_ref,
):
    steps, levels, cells, block, groups, tracers, stride = dims
    width = 128
    tiles = lax.axis_size("tile")
    here = lax.axis_index("tile")
    low_flip = flip_ref[lax.rem(here + tiles - 1, tiles)]
    high_flip = flip_ref[here]

    lane = lax.broadcasted_iota(jnp.int32, (8, width), 1)
    row = lax.broadcasted_iota(jnp.int32, (8, width), 0)
    first_row = row == 0
    last_row = row == groups - 1

    def order_of(flip):
        return jnp.where(flip == 1, width - 1 - lane, lane)

    low_order = order_of(low_flip)
    high_order = order_of(high_flip)
    low_sign = jnp.where(low_flip == 1, -1.0, 1.0).astype(jnp.float32)
    high_sign = jnp.where(high_flip == 1, -1.0, 1.0).astype(jnp.float32)

    def turned(values, order):
        return jnp.take_along_axis(values, order, axis=1)

    def shift(values, by):
        return pltpu.roll(values, by % width, 1)

    def coefficients(level):
        gain_a = gain_a_ref[level]
        gain_b = gain_b_ref[level]
        refs = (met_low_ref, met_own_ref, met_high_ref)
        orders = (low_order, None, high_order)
        signs = (low_sign, None, high_sign)
        mass = None
        pressures = [
            [
                [refs[t][pl.ds(2 * steps * levels * block + s * block + c, 8, stride=stride), :] for c in range(block)]
                for t in range(3)
            ]
            for s in range(steps)
        ]
        for s in range(steps):
            flux_x = [[None] * block for _ in range(3)]
            flux_y = [[None] * block for _ in range(3)]
            start = [[None] * block for _ in range(3)]
            for t in range(3):
                for c in range(block):
                    at = s * levels * block + level * block + c
                    met = gain_a + gain_b * pressures[s][t][c]
                    x = refs[t][pl.ds(at, 8, stride=stride), :] * met
                    y = refs[t][pl.ds(steps * levels * block + at, 8, stride=stride), :] * met
                    if orders[t] is not None:
                        x = turned(x, orders[t])
                        y = turned(y, orders[t]) * signs[t]
                        if s == 0:
                            met = turned(met, orders[t])
                    flux_x[t][c] = x
                    flux_y[t][c] = y
                    if s == 0:
                        start[t][c] = met
            if s == 0:
                mass = start
            face_x = [[None] * block for _ in range(3)]
            for t in range(3):
                for c in range(block):
                    if c:
                        before = flux_x[t][c - 1]
                    else:
                        before = pltpu.roll(flux_x[t][block - 1], 1, 0)
                        if t:
                            before = jnp.where(first_row, pltpu.roll(flux_x[t - 1][block - 1], 1, 0), before)
                    face_x[t][c] = 0.5 * (before + flux_x[t][c])
            for t in range(3):
                for c in range(block):
                    if c < block - 1:
                        after = face_x[t][c + 1]
                    else:
                        after = pltpu.roll(face_x[t][0], groups - 1, 0)
                        if t < 2:
                            after = jnp.where(last_row, pltpu.roll(face_x[t + 1][0], groups - 1, 0), after)
                    face_y = jnp.where(lane == 0, 0.0, 0.5 * (shift(flux_y[t][c], 1) + flux_y[t][c]))
                    div = (after - face_x[t][c]) + (shift(face_y, -1) - face_y)
                    rows = pl.ds(t * cells + c, 8, stride=block)
                    flux_x_ref[s, rows, :] = face_x[t][c] * (1.0 / 30.0)
                    scaled = face_y * (1.0 / 30.0)
                    up = jnp.maximum(scaled, 0.0)
                    down = jnp.minimum(scaled, 0.0)
                    k0 = up
                    k1 = -6.5 * up - 1.5 * down
                    k2 = 23.5 * up + 13.5 * down
                    k3 = 13.5 * up + 23.5 * down
                    k4 = -1.5 * up - 6.5 * down
                    k5 = down
                    k2 = jnp.where(lane == 1, k2 + k1 + k0, k2)
                    k1 = jnp.where(lane == 1, 0.0, jnp.where(lane == 2, k1 + k0, k1))
                    k0 = jnp.where(lane <= 2, 0.0, k0)
                    k3 = jnp.where(lane == width - 1, k3 + k4 + k5, k3)
                    k4 = jnp.where(lane == width - 1, 0.0, jnp.where(lane == width - 2, k4 + k5, k4))
                    k5 = jnp.where(lane >= width - 2, 0.0, k5)
                    for index, value in enumerate((k0, k1, k2, k3, k4, k5)):
                        band_ref[s, index, rows, :] = value
                    mass_row_ref[s, rows, :] = mass[t][c]
                    for index, weight in enumerate(SECTION_WEIGHTS):
                        after_mass = mass[t][c] - weight * div
                        inverse_ref[s, index, rows, :] = weight / after_mass
                    mass[t][c] = mass[t][c] - div
        for c in range(block):
            mass_ref[pl.ds(level * cells + c, 8, stride=block), :] = mass[1][c]

    def spread(ref, lead, at):
        return jnp.broadcast_to(ref[lead + (pl.ds(at, 1), slice(None))], (8, width))

    def section(s, number, low, count, positive, source, store):
        weight = SECTION_WEIGHTS[number]
        held = {}

        def q(offset):
            if offset not in held:
                held[offset] = source[low + offset]
            return held[offset]

        def along_x(face):
            flux = spread(flux_x_ref, (s,), low + face)
            if positive:
                five = (q(face - 3), q(face - 2), q(face - 1), q(face), q(face + 1))
            else:
                five = (q(face + 2), q(face + 1), q(face), q(face - 1), q(face - 2))
            a, b, c, d, e = five
            return flux * (((a - 6.5 * b) + (23.5 * c + 13.5 * d)) - 1.5 * e)

        before = along_x(0)
        for k in range(count):
            after = along_x(k + 1)
            here_q = q(k)
            terms = []
            for index in range(6):
                moved = here_q if index == 3 else shift(here_q, 3 - index)
                terms.append(spread(band_ref, (s, index), low + k) * moved)
            along_y = ((terms[0] + terms[1]) + (terms[2] + terms[3])) + (terms[4] + terms[5])
            div = (after - before) + (shift(along_y, -1) - along_y)
            if number == 0:
                start = here_q * spread(mass_row_ref, (s,), low + k)
                start_ref[low + k] = start
            else:
                start = start_ref[low + k]
            if weight != 1.0:
                start = start * (1.0 / weight)
            store(low + k, k, (start - div) * spread(inverse_ref, (s, number), low + k))
            before = after
            held.pop(k - 3, None)

    def level_body(level, carry):
        coefficients(level)
        for r in range(6, 24):
            at = pl.ds(level * cells + r, tracers, stride=levels * cells)
            q_a[r] = turned(low_ref[at, :], low_order)
        for r in range(cells):
            at = pl.ds(level * cells + r, tracers, stride=levels * cells)
            q_a[cells + r] = own_ref[at, :]
        for r in range(18):
            at = pl.ds(level * cells + r, tracers, stride=levels * cells)
            q_a[2 * cells + r] = turned(high_ref[at, :], high_order)

        reach = [jnp.where(sign_ref[s, level] > 0.0, 3, 2).astype(jnp.int32) for s in range(steps)]
        total = steps * 3
        lows = [None] * total
        lows[total - 1] = jnp.int32(cells)
        for n in range(total - 2, -1, -1):
            lows[n] = lows[n + 1] - reach[(n + 1) // 3]

        def out_store(at, k, value):
            out_ref[pl.ds(level * cells + k, tracers, stride=levels * cells), :] = value

        def into(ref):
            def store(at, k, value):
                ref[at] = value

            return store

        for s in range(steps):
            for positive in (True, False):

                @pl.when((sign_ref[s, level] > 0.0) == positive)
                def _():
                    last = out_store if s == steps - 1 else into(q_a)
                    plan = ((q_a, into(q_b)), (q_b, into(q_c)), (q_c, last))
                    for number, (source, store) in enumerate(plan):
                        n = s * 3 + number
                        section(s, number, lows[n], cells + 5 * (total - 1 - n), positive, source, store)

        return carry

    lax.fori_loop(0, levels, level_body, 0)


def local(tracers, wind_x, wind_y, surface_p, coef_a, coef_b, edge_flip):
    count, levels, cells, width = tracers.shape
    steps, block = wind_x.shape[0], wind_x.shape[3]
    groups, tiles = lax.axis_size("grp"), lax.axis_size("tile")
    used = (2 * levels + 1) * steps * block
    stride = -(-used // 8) * 8

    signs = wind_x[:, :, 0, 0, 0]
    packed = jnp.concatenate(
        [wind_x.reshape(-1, width), wind_y.reshape(-1, width), surface_p.reshape(-1, width)], axis=0
    )
    packed = jnp.pad(packed, ((0, stride - used), (0, 0)))
    low = lax.ppermute(tracers, "tile", ring(tiles, 1))
    high = lax.ppermute(tracers, "tile", ring(tiles, -1))
    met = lax.all_to_all(jnp.broadcast_to(packed[None], (groups, stride, width)), "grp", 0, 0, tiled=True)
    met_low = lax.ppermute(met, "tile", ring(tiles, 1))
    met_high = lax.ppermute(met, "tile", ring(tiles, -1))

    flat = (count * levels * cells, width)
    met_flat = (groups * stride, width)
    dims = (steps, levels, cells, block, groups, count, stride)
    rows = 3 * cells
    smem = pl.BlockSpec(memory_space=pltpu.SMEM)
    vmem = pl.BlockSpec(memory_space=pltpu.VMEM)
    out, mass = pl.pallas_call(
        functools.partial(advect_kernel, dims),
        out_shape=(
            jax.ShapeDtypeStruct(flat, jnp.float32),
            jax.ShapeDtypeStruct((levels * cells, width), jnp.float32),
        ),
        in_specs=[smem] * 4 + [vmem] * 6,
        out_specs=(vmem, vmem),
        scratch_shapes=[pltpu.VMEM((rows, count, width), jnp.float32)] * 4
        + [
            pltpu.VMEM((steps, rows, width), jnp.float32),
            pltpu.VMEM((steps, 6, rows, width), jnp.float32),
            pltpu.VMEM((steps, 3, rows, width), jnp.float32),
            pltpu.VMEM((steps, rows, width), jnp.float32),
        ],
        compiler_params=pltpu.CompilerParams(vmem_limit_bytes=VMEM_LIMIT),
        name="advect",
    )(
        signs,
        edge_flip,
        coef_a,
        coef_b,
        tracers.reshape(flat),
        low.reshape(flat),
        high.reshape(flat),
        met.reshape(met_flat),
        met_low.reshape(met_flat),
        met_high.reshape(met_flat),
    )
    return out.reshape(tracers.shape), mass.reshape(levels, cells, width)


def solution(mesh):
    return jax.shard_map(
        local,
        mesh=mesh,
        in_specs=(
            P("grp", None, "tile", None),
            P(None, None, "tile", "grp", None),
            P(None, None, "tile", "grp", None),
            P(None, "tile", "grp", None),
            P(),
            P(),
            P(),
        ),
        out_specs=(P("grp", None, "tile", None), P(None, "tile", None)),
        check_vma=False,
    )
```

```python
import functools

import jax
import jax.numpy as jnp
import ml_dtypes
import numpy as np
from jax import lax
from jax.experimental import pallas as pl
from jax.experimental.pallas import tpu as pltpu
from jax.sharding import PartitionSpec as P

SECTION_WEIGHTS = (1.0 / 3.0, 0.5, 1.0)
TOGETHER = 3
SLOTS = 32
VMEM_LIMIT = 48 * 1024 * 1024


def ring(count, step):
    return [(i, (i + step) % count) for i in range(count)]


def stencil_weights(width):
    out = np.zeros((2, 2 * width, 2 * width), np.float32)
    for side in range(2):
        for j in range(width):
            face = j + side
            for tap, value in enumerate((2.0, -13.0, 47.0, 27.0, -3.0)):
                up = min(max(face - 3 + tap, 0), width - 1)
                down = min(max(face + 2 - tap, 0), width - 1)
                for half in (0, width):
                    out[side, half + up, j] += value
                    out[side, half + down, width + j] += value
    return out.astype(ml_dtypes.bfloat16)


def advect_kernel(
    dims,
    sign_ref,
    flip_ref,
    gain_a_ref,
    gain_b_ref,
    own_ref,
    low_ref,
    high_ref,
    met_own_ref,
    met_low_ref,
    met_high_ref,
    weights_ref,
    out_ref,
    mass_ref,
    q_a,
    q_b,
    q_c,
    q_d,
    start_ref,
    coef_ref,
):
    steps, levels, cells, block, groups, tracers, stride = dims
    width = 128
    rows = 3 * cells
    tiles = lax.axis_size("tile")
    here = lax.axis_index("tile")
    low_flip = flip_ref[lax.rem(here + tiles - 1, tiles)]
    high_flip = flip_ref[here]

    lane = lax.broadcasted_iota(jnp.int32, (8, width), 1)
    row = lax.broadcasted_iota(jnp.int32, (8, width), 0)
    first_row = row == 0
    last_row = row == groups - 1

    def order_of(flip):
        return jnp.where(flip == 1, width - 1 - lane, lane)

    low_order = order_of(low_flip)
    high_order = order_of(high_flip)
    low_sign = jnp.where(low_flip == 1, -1.0, 1.0).astype(jnp.float32)
    high_sign = jnp.where(high_flip == 1, -1.0, 1.0).astype(jnp.float32)

    def turned(values, order):
        return jnp.take_along_axis(values, order, axis=1)

    def shift(values, by):
        return pltpu.roll(values, by % width, 1)

    def coefficients(level, slot):
        gain_a = gain_a_ref[level]
        gain_b = gain_b_ref[level]
        refs = (met_low_ref, met_own_ref, met_high_ref)
        orders = (low_order, None, high_order)
        signs = (low_sign, None, high_sign)
        mass = None
        for s in range(steps):
            flux_x = [[None] * block for _ in range(3)]
            flux_y = [[None] * block for _ in range(3)]
            start = [[None] * block for _ in range(3)]
            for t in range(3):
                for c in range(block):
                    at = s * levels * block + level * block + c
                    pressure = refs[t][pl.ds(2 * steps * levels * block + s * block + c, 8, stride=stride), :]
                    met = gain_a + gain_b * pressure
                    x = refs[t][pl.ds(at, 8, stride=stride), :] * met
                    y = refs[t][pl.ds(steps * levels * block + at, 8, stride=stride), :] * met
                    if orders[t] is not None:
                        x = turned(x, orders[t])
                        y = turned(y, orders[t]) * signs[t]
                        if s == 0:
                            met = turned(met, orders[t])
                    flux_x[t][c] = x
                    flux_y[t][c] = y
                    start[t][c] = met
            if s == 0:
                mass = start
            face_x = [[None] * block for _ in range(3)]
            for t in range(3):
                for c in range(block):
                    if c:
                        before = flux_x[t][c - 1]
                    else:
                        before = pltpu.roll(flux_x[t][block - 1], 1, 0)
                        if t:
                            before = jnp.where(first_row, pltpu.roll(flux_x[t - 1][block - 1], 1, 0), before)
                    face_x[t][c] = 0.5 * (before + flux_x[t][c])
            for t in range(3):
                for c in range(block):
                    if c < block - 1:
                        after = face_x[t][c + 1]
                    else:
                        after = pltpu.roll(face_x[t][0], groups - 1, 0)
                        if t < 2:
                            after = jnp.where(last_row, pltpu.roll(face_x[t + 1][0], groups - 1, 0), after)
                    face_y = jnp.where(lane == 0, 0.0, 0.5 * (shift(flux_y[t][c], 1) + flux_y[t][c]))
                    next_y = shift(face_y, -1)
                    div = (after - face_x[t][c]) + (next_y - face_y)
                    kinds = [jnp.abs(face_x[t][c]) * (1.0 / 30.0), face_y * (1.0 / 60.0), next_y * (1.0 / 60.0)]
                    for weight in SECTION_WEIGHTS:
                        kinds.append(weight / (mass[t][c] - weight * div))
                    kinds.append(mass[t][c])
                    for kind, value in enumerate(kinds):
                        coef_ref[slot, s, pl.ds((t * cells + c) * 8 + kind, 8, stride=8 * block), :] = value
                    mass[t][c] = mass[t][c] - div
        for c in range(block):
            mass_ref[pl.ds(level * cells + c, 8, stride=block), :] = mass[1][c]

    def run(*accs):
        for side in range(2):
            pltpu.matmul_push_rhs(weights_ref[side], 0, side)
        for side in range(2):
            pltpu.matmul_acc_lhs(accs[side], jnp.zeros((16, 256), jnp.bfloat16), load_staged_rhs=0)
            out_ref[0:16, :] = pltpu.matmul_pop(accs[side])[:, :width]

        def group_body(group, carry):
            flow = []
            for slot in range(TOGETHER):
                level = group * TOGETHER + slot
                coefficients(level, slot)
                ahead = [sign_ref[s, level] > 0.0 for s in range(steps)]
                way = [jnp.where(a, 1, -1).astype(jnp.int32) for a in ahead]
                same = way[0] == way[1]
                first = jnp.where(same, cells - 9, cells - 6)
                inlet = [first - 6, jnp.int32(cells - 6)]
                base = [jnp.where(a, p, rows - 1 - p) for a, p in zip(ahead, inlet)]
                for r in range(6, rows - 6):
                    ref, order = ((low_ref, low_order), (own_ref, None), (high_ref, high_order))[r // cells]
                    value = ref[pl.ds(level * cells + r % cells, tracers, stride=levels * cells), :]
                    if order is not None:
                        value = turned(value, order)
                    q_a[slot, (r - base[0]) * way[0] + 6] = value
                flow.append((level, ahead, way, same, base))

            plan = [
                (0, 0, q_a, 3, q_b),
                (0, 1, q_b, 0, q_c),
                (0, 2, q_c, 0, q_d),
                (1, 0, q_d, 0, q_b),
                (1, 1, q_b, 0, q_c),
                (1, 2, q_c, 0, None),
            ]
            items = [(n, slot) for n in range(6) for slot in range(TOGETHER)]
            counts = [cells + 5 * (5 - n) for n in range(6)]
            parts = [-(-c // 2) for c in counts]
            pushed, popped = [0], [0]

            def push(item, part):
                n, slot = item
                _, _, source, pad, _ = plan[n]
                at = 2 * part + 3 + pad
                both = jnp.concatenate([source[slot, at], source[slot, at + 1]], axis=0)
                high = both.astype(jnp.bfloat16)
                rest = (both - high.astype(jnp.float32)).astype(jnp.bfloat16)
                lhs = jnp.concatenate([high, rest], axis=1)
                place = pushed[0] % SLOTS
                pushed[0] += 1
                for side in range(2):
                    pltpu.matmul_acc_lhs(accs[2 * place + side], lhs)

            state = {}

            def finish(item, part):
                n, slot = item
                s, number, source, pad, target = plan[n]
                level, ahead, way, same, base = flow[slot]
                weight = SECTION_WEIGHTS[number]
                place = popped[0] % SLOTS
                popped[0] += 1
                pops = [pltpu.matmul_pop(accs[2 * place + side]) for side in range(2)]
                if part == 0:
                    state.clear()

                def spot(k):
                    return base[s] + way[s] * (k + 3 * number)

                def spread(at, kind):
                    return jnp.broadcast_to(coef_ref[slot, s, pl.ds(at * 8 + kind, 1), :], (8, width))

                def q(k):
                    if k not in state:
                        state[k] = source[slot, k + pad]
                    return state[k]

                def along_x(k):
                    at = spot(k) + jnp.where(ahead[s], 0, 1)
                    five = ((q(k) - 6.5 * q(k + 1)) + (23.5 * q(k + 2) + 13.5 * q(k + 3))) - 1.5 * q(k + 4)
                    return spread(at, 0) * five

                if part == 0:
                    state["before"] = along_x(0)
                for half in range(2):
                    k = 2 * part + half
                    if k >= counts[n]:
                        continue
                    at = spot(k)
                    after = along_x(k + 1)
                    sides = []
                    for side in range(2):
                        flux = spread(at, 1 + side)
                        rows_of = pops[side][8 * half : 8 * half + 8]
                        sides.append(flux * jnp.where(flux >= 0.0, rows_of[:, :width], rows_of[:, width:]))
                    div = (after - state["before"]) + (sides[1] - sides[0])
                    if number == 0:
                        start = q(k + 3) * spread(at, 6)
                        start_ref[slot, k] = start
                    else:
                        start = start_ref[slot, k + 3 * number]
                    if weight != 1.0:
                        start = start * (1.0 / weight)
                    value = (start - div) * spread(at, 3 + number)
                    if target is None:
                        i = jnp.where(ahead[1], k, cells - 1 - k)
                        out_ref[pl.ds(level * cells + i, tracers, stride=levels * cells), :] = value
                    elif target is q_d:
                        q_d[slot, jnp.where(same, k, counts[n] - 1 - k)] = value
                    else:
                        target[slot, k] = value
                    state["before"] = after
                    state.pop(k, None)

            for part in range(parts[0]):
                push(items[0], part)
            for index, item in enumerate(items):
                following = items[index + 1] if index + 1 < len(items) else None
                ahead_parts = parts[following[0]] if following else 0
                for part in range(max(parts[item[0]], ahead_parts)):
                    if part < parts[item[0]]:
                        finish(item, part)
                    if part < ahead_parts:
                        push(following, part)
            return carry

        lax.fori_loop(0, levels // TOGETHER, group_body, 0)

    acc = [pltpu.ACC(side)((16, 256), jnp.float32) for _ in range(SLOTS) for side in range(2)]
    pl.run_scoped(run, *acc)


def local(tracers, wind_x, wind_y, surface_p, coef_a, coef_b, edge_flip):
    count, levels, cells, width = tracers.shape
    steps, block = wind_x.shape[0], wind_x.shape[3]
    groups, tiles = lax.axis_size("grp"), lax.axis_size("tile")
    used = (2 * levels + 1) * steps * block
    stride = -(-used // 8) * 8

    signs = wind_x[:, :, 0, 0, 0]
    packed = jnp.concatenate(
        [wind_x.reshape(-1, width), wind_y.reshape(-1, width), surface_p.reshape(-1, width)], axis=0
    )
    packed = jnp.pad(packed, ((0, stride - used), (0, 0)))
    low = lax.ppermute(tracers, "tile", ring(tiles, 1))
    high = lax.ppermute(tracers, "tile", ring(tiles, -1))
    met = lax.all_to_all(jnp.broadcast_to(packed[None], (groups, stride, width)), "grp", 0, 0, tiled=True)
    met_low = lax.ppermute(met, "tile", ring(tiles, 1))
    met_high = lax.ppermute(met, "tile", ring(tiles, -1))

    flat = (count * levels * cells, width)
    met_flat = (groups * stride, width)
    dims = (steps, levels, cells, block, groups, count, stride)
    rows = 3 * cells
    smem = pl.BlockSpec(memory_space=pltpu.SMEM)
    vmem = pl.BlockSpec(memory_space=pltpu.VMEM)
    out, mass = pl.pallas_call(
        functools.partial(advect_kernel, dims),
        out_shape=(
            jax.ShapeDtypeStruct(flat, jnp.float32),
            jax.ShapeDtypeStruct((levels * cells, width), jnp.float32),
        ),
        in_specs=[smem] * 4 + [vmem] * 7,
        out_specs=(vmem, vmem),
        scratch_shapes=[
            pltpu.VMEM((TOGETHER, 64, count, width), jnp.float32),
            pltpu.VMEM((TOGETHER, 56, count, width), jnp.float32),
            pltpu.VMEM((TOGETHER, 56, count, width), jnp.float32),
            pltpu.VMEM((TOGETHER, 40, count, width), jnp.float32),
            pltpu.VMEM((TOGETHER, 56, count, width), jnp.float32),
            pltpu.VMEM((TOGETHER, steps, rows * 8, width), jnp.float32),
        ],
        compiler_params=pltpu.CompilerParams(vmem_limit_bytes=VMEM_LIMIT),
        name="advect",
    )(
        signs,
        edge_flip,
        coef_a,
        coef_b,
        tracers.reshape(flat),
        low.reshape(flat),
        high.reshape(flat),
        met.reshape(met_flat),
        met_low.reshape(met_flat),
        met_high.reshape(met_flat),
        jnp.asarray(stencil_weights(width)),
    )
    return out.reshape(tracers.shape), mass.reshape(levels, cells, width)


def solution(mesh):
    return jax.shard_map(
        local,
        mesh=mesh,
        in_specs=(
            P("grp", None, "tile", None),
            P(None, None, "tile", "grp", None),
            P(None, None, "tile", "grp", None),
            P(None, "tile", "grp", None),
            P(),
            P(),
            P(),
        ),
        out_specs=(P("grp", None, "tile", None), P(None, "tile", None)),
        check_vma=False,
    )
```

```python
import functools

import jax
import jax.numpy as jnp
import ml_dtypes
import numpy as np
from jax import lax
from jax.experimental import pallas as pl
from jax.experimental.pallas import tpu as pltpu
from jax.sharding import PartitionSpec as P

SECTION_WEIGHTS = (1.0 / 3.0, 0.5, 1.0)
TOGETHER = 3
SLOTS = 32
VMEM_LIMIT = 48 * 1024 * 1024


def ring(count, step):
    return [(i, (i + step) % count) for i in range(count)]


def stencil_weights(width):
    out = np.zeros((2, 2 * width, 2 * width), np.float32)
    for side in range(2):
        for j in range(width):
            face = j + side
            for tap, value in enumerate((2.0, -13.0, 47.0, 27.0, -3.0)):
                up = min(max(face - 3 + tap, 0), width - 1)
                down = min(max(face + 2 - tap, 0), width - 1)
                for half in (0, width):
                    out[side, half + up, j] += value
                    out[side, half + down, width + j] += value
    return out.astype(ml_dtypes.bfloat16)


def advect_kernel(
    dims,
    sign_ref,
    flip_ref,
    gain_a_ref,
    gain_b_ref,
    own_ref,
    low_ref,
    high_ref,
    met_own_ref,
    met_low_ref,
    met_high_ref,
    weights_ref,
    out_ref,
    mass_ref,
    q_a,
    q_b,
    q_c,
    q_d,
    start_ref,
    coef_ref,
):
    steps, levels, cells, block, groups, tracers, stride = dims
    width = 128
    rows = 3 * cells
    tiles = lax.axis_size("tile")
    here = lax.axis_index("tile")
    low_flip = flip_ref[lax.rem(here + tiles - 1, tiles)]
    high_flip = flip_ref[here]

    lane = lax.broadcasted_iota(jnp.int32, (8, width), 1)
    row = lax.broadcasted_iota(jnp.int32, (8, width), 0)
    first_row = row == 0
    last_row = row == groups - 1

    def order_of(flip):
        return jnp.where(flip == 1, width - 1 - lane, lane)

    low_order = order_of(low_flip)
    high_order = order_of(high_flip)
    low_sign = jnp.where(low_flip == 1, -1.0, 1.0).astype(jnp.float32)
    high_sign = jnp.where(high_flip == 1, -1.0, 1.0).astype(jnp.float32)

    def turned(values, order):
        return jnp.take_along_axis(values, order, axis=1)

    def shift(values, by):
        return pltpu.roll(values, by % width, 1)

    def coefficients(level, slot):
        gain_a = gain_a_ref[level]
        gain_b = gain_b_ref[level]
        refs = (met_low_ref, met_own_ref, met_high_ref)
        orders = (low_order, None, high_order)
        signs = (low_sign, None, high_sign)
        mass = None
        for s in range(steps):
            flux_x = [[None] * block for _ in range(3)]
            flux_y = [[None] * block for _ in range(3)]
            start = [[None] * block for _ in range(3)]
            for t in range(3):
                for c in range(block):
                    at = s * levels * block + level * block + c
                    pressure = refs[t][pl.ds(112 + s * block + c, 8, stride=stride), :]
                    met = gain_a + gain_b * pressure
                    x = refs[t][pl.ds(at, 8, stride=stride), :] * met
                    y = refs[t][pl.ds(56 + at, 8, stride=stride), :] * met
                    if orders[t] is not None:
                        x = turned(x, orders[t])
                        y = turned(y, orders[t]) * signs[t]
                        if s == 0:
                            met = turned(met, orders[t])
                    flux_x[t][c] = x
                    flux_y[t][c] = y
                    start[t][c] = met
            if s == 0:
                mass = start
            face_x = [[None] * block for _ in range(3)]
            for t in range(3):
                for c in range(block):
                    if c:
                        before = flux_x[t][c - 1]
                    else:
                        before = pltpu.roll(flux_x[t][block - 1], 1, 0)
                        if t:
                            before = jnp.where(first_row, pltpu.roll(flux_x[t - 1][block - 1], 1, 0), before)
                    face_x[t][c] = 0.5 * (before + flux_x[t][c])
            for t in range(3):
                for c in range(block):
                    if c < block - 1:
                        after = face_x[t][c + 1]
                    else:
                        after = pltpu.roll(face_x[t][0], groups - 1, 0)
                        if t < 2:
                            after = jnp.where(last_row, pltpu.roll(face_x[t + 1][0], groups - 1, 0), after)
                    face_y = jnp.where(lane == 0, 0.0, 0.5 * (shift(flux_y[t][c], 1) + flux_y[t][c]))
                    next_y = shift(face_y, -1)
                    div = (after - face_x[t][c]) + (next_y - face_y)
                    kinds = [jnp.abs(face_x[t][c]) * (1.0 / 30.0), face_y * (1.0 / 60.0), next_y * (1.0 / 60.0)]
                    for weight in SECTION_WEIGHTS:
                        kinds.append(weight / (mass[t][c] - weight * div))
                    kinds.append(mass[t][c])
                    for kind, value in enumerate(kinds):
                        coef_ref[slot, s, pl.ds((t * cells + c) * 8 + kind, 8, stride=8 * block), :] = value
                    mass[t][c] = mass[t][c] - div
        for c in range(block):
            mass_ref[pl.ds(level * cells + c, 8, stride=block), :] = mass[1][c]

    def run(*accs):
        for side in range(2):
            pltpu.matmul_push_rhs(weights_ref[side], 0, side)
        for side in range(2):
            pltpu.matmul_acc_lhs(accs[side], jnp.zeros((16, 256), jnp.bfloat16), load_staged_rhs=0)
            out_ref[0:16, :] = pltpu.matmul_pop(accs[side])[:, :width]

        def group_body(group, carry):
            flow = []
            for slot in range(TOGETHER):
                level = group * TOGETHER + slot
                coefficients(level, slot)
                ahead = [sign_ref[s, level] > 0.0 for s in range(steps)]
                way = [jnp.where(a, 1, -1).astype(jnp.int32) for a in ahead]
                same = way[0] == way[1]
                first = jnp.where(same, cells - 9, cells - 6)
                inlet = [first - 6, jnp.int32(cells - 6)]
                base = [jnp.where(a, p, rows - 1 - p) for a, p in zip(ahead, inlet)]
                for r in range(6, rows - 6):
                    if r < cells:
                        at = (level * 18 + r - 6) * tracers
                        value = turned(low_ref[pl.ds(pl.multiple_of(at, 8), tracers), :], low_order)
                    elif r < 2 * cells:
                        value = own_ref[pl.ds(level * cells + r - cells, tracers, stride=levels * cells), :]
                    else:
                        at = (level * 18 + r - 2 * cells) * tracers
                        value = turned(high_ref[pl.ds(pl.multiple_of(at, 8), tracers), :], high_order)
                    q_a[slot, (r - base[0]) * way[0] + 6] = value
                flow.append((level, ahead, way, same, base))

            plan = [
                (0, 0, q_a, 3, q_b),
                (0, 1, q_b, 0, q_c),
                (0, 2, q_c, 0, q_d),
                (1, 0, q_d, 0, q_b),
                (1, 1, q_b, 0, q_c),
                (1, 2, q_c, 0, None),
            ]
            items = [(n, slot) for n in range(6) for slot in range(TOGETHER)]
            counts = [cells + 5 * (5 - n) for n in range(6)]
            parts = [-(-c // 2) for c in counts]
            pushed, popped = [0], [0]

            def push(item, part):
                n, slot = item
                _, _, source, pad, _ = plan[n]
                at = 2 * part + 3 + pad
                both = jnp.concatenate([source[slot, at], source[slot, at + 1]], axis=0)
                high = both.astype(jnp.bfloat16)
                rest = (both - high.astype(jnp.float32)).astype(jnp.bfloat16)
                lhs = jnp.concatenate([high, rest], axis=1)
                place = pushed[0] % SLOTS
                pushed[0] += 1
                for side in range(2):
                    pltpu.matmul_acc_lhs(accs[2 * place + side], lhs)

            state = {}

            def finish(item, part):
                n, slot = item
                s, number, source, pad, target = plan[n]
                level, ahead, way, same, base = flow[slot]
                weight = SECTION_WEIGHTS[number]
                place = popped[0] % SLOTS
                popped[0] += 1
                pops = [pltpu.matmul_pop(accs[2 * place + side]) for side in range(2)]
                if part == 0:
                    state.clear()

                def spot(k):
                    return base[s] + way[s] * (k + 3 * number)

                def spread(at, kind):
                    return jnp.broadcast_to(coef_ref[slot, s, pl.ds(at * 8 + kind, 1), :], (8, width))

                def q(k):
                    if k not in state:
                        state[k] = source[slot, k + pad]
                    return state[k]

                def along_x(k):
                    at = spot(k) + jnp.where(ahead[s], 0, 1)
                    five = ((q(k) - 6.5 * q(k + 1)) + (23.5 * q(k + 2) + 13.5 * q(k + 3))) - 1.5 * q(k + 4)
                    return spread(at, 0) * five

                if part == 0:
                    state["before"] = along_x(0)
                for half in range(2):
                    k = 2 * part + half
                    if k >= counts[n]:
                        continue
                    at = spot(k)
                    after = along_x(k + 1)
                    sides = []
                    for side in range(2):
                        flux = spread(at, 1 + side)
                        rows_of = pops[side][8 * half : 8 * half + 8]
                        sides.append(flux * jnp.where(flux >= 0.0, rows_of[:, :width], rows_of[:, width:]))
                    div = (after - state["before"]) + (sides[1] - sides[0])
                    if number == 0:
                        start = q(k + 3) * spread(at, 6)
                        start_ref[slot, k] = start
                    else:
                        start = start_ref[slot, k + 3 * number]
                    if weight != 1.0:
                        start = start * (1.0 / weight)
                    value = (start - div) * spread(at, 3 + number)
                    if target is None:
                        i = jnp.where(ahead[1], k, cells - 1 - k)
                        out_ref[pl.ds(level * cells + i, tracers, stride=levels * cells), :] = value
                    elif target is q_d:
                        q_d[slot, jnp.where(same, k, counts[n] - 1 - k)] = value
                    else:
                        target[slot, k] = value
                    state["before"] = after
                    state.pop(k, None)

            for part in range(parts[0]):
                push(items[0], part)
            for index, item in enumerate(items):
                following = items[index + 1] if index + 1 < len(items) else None
                ahead_parts = parts[following[0]] if following else 0
                for part in range(max(parts[item[0]], ahead_parts)):
                    if part < parts[item[0]]:
                        finish(item, part)
                    if part < ahead_parts:
                        push(following, part)
            return carry

        lax.fori_loop(0, levels // TOGETHER, group_body, 0)

    acc = [pltpu.ACC(side)((16, 256), jnp.float32) for _ in range(SLOTS) for side in range(2)]
    pl.run_scoped(run, *acc)


def edge_kernel(levels, cells, tracers, field_ref, up_ref, down_ref):
    def level_body(level, carry):
        for r in range(18):
            at = pl.ds(pl.multiple_of((level * 18 + r) * tracers, 8), tracers)
            up_ref[at, :] = field_ref[pl.ds(level * cells + cells - 18 + r, tracers, stride=levels * cells), :]
            down_ref[at, :] = field_ref[pl.ds(level * cells + r, tracers, stride=levels * cells), :]
        return carry

    lax.fori_loop(0, levels, level_body, 0)


def met_kernel(groups, x_ref, y_ref, p_ref, out_ref):
    for ref, first in ((x_ref, 0), (y_ref, 56), (p_ref, 112)):
        count = ref.shape[0]
        value = ref[...].reshape(count, ref.shape[2])
        for g in range(groups):
            out_ref[g, first : first + count, :] = value


def local(tracers, wind_x, wind_y, surface_p, coef_a, coef_b, edge_flip):
    count, levels, cells, width = tracers.shape
    steps, block = wind_x.shape[0], wind_x.shape[3]
    groups, tiles = lax.axis_size("grp"), lax.axis_size("tile")
    stride = 120
    smem = pl.BlockSpec(memory_space=pltpu.SMEM)
    vmem = pl.BlockSpec(memory_space=pltpu.VMEM)
    flat = (count * levels * cells, width)
    edge = jax.ShapeDtypeStruct((levels * 18 * count, width), jnp.float32)

    signs = wind_x[:, :, 0, 0, 0]
    up, down = pl.pallas_call(
        functools.partial(edge_kernel, levels, cells, count),
        out_shape=(edge, edge),
        in_specs=[vmem],
        out_specs=(vmem, vmem),
        name="edges",
    )(tracers.reshape(flat))
    low = lax.ppermute(up, "tile", ring(tiles, 1))
    high = lax.ppermute(down, "tile", ring(tiles, -1))
    packed = pl.pallas_call(
        functools.partial(met_kernel, groups),
        out_shape=jax.ShapeDtypeStruct((groups, stride, width), jnp.float32),
        in_specs=[vmem] * 3,
        out_specs=vmem,
        name="met",
    )(wind_x.reshape(-1, 1, width), wind_y.reshape(-1, 1, width), surface_p.reshape(-1, 1, width))
    met = lax.all_to_all(packed, "grp", 0, 0, tiled=True)
    met_low = lax.ppermute(met, "tile", ring(tiles, 1))
    met_high = lax.ppermute(met, "tile", ring(tiles, -1))

    met_flat = (groups * stride, width)
    dims = (steps, levels, cells, block, groups, count, stride)
    rows = 3 * cells
    out, mass = pl.pallas_call(
        functools.partial(advect_kernel, dims),
        out_shape=(
            jax.ShapeDtypeStruct(flat, jnp.float32),
            jax.ShapeDtypeStruct((levels * cells, width), jnp.float32),
        ),
        in_specs=[smem] * 4 + [vmem] * 7,
        out_specs=(vmem, vmem),
        scratch_shapes=[
            pltpu.VMEM((TOGETHER, 64, count, width), jnp.float32),
            pltpu.VMEM((TOGETHER, 56, count, width), jnp.float32),
            pltpu.VMEM((TOGETHER, 56, count, width), jnp.float32),
            pltpu.VMEM((TOGETHER, 40, count, width), jnp.float32),
            pltpu.VMEM((TOGETHER, 56, count, width), jnp.float32),
            pltpu.VMEM((TOGETHER, steps, rows * 8, width), jnp.float32),
        ],
        compiler_params=pltpu.CompilerParams(vmem_limit_bytes=VMEM_LIMIT),
        name="advect",
    )(
        signs,
        edge_flip,
        coef_a,
        coef_b,
        tracers.reshape(flat),
        low,
        high,
        met.reshape(met_flat),
        met_low.reshape(met_flat),
        met_high.reshape(met_flat),
        jnp.asarray(stencil_weights(width)),
    )
    return out.reshape(tracers.shape), mass.reshape(levels, cells, width)


def solution(mesh):
    return jax.shard_map(
        local,
        mesh=mesh,
        in_specs=(
            P("grp", None, "tile", None),
            P(None, None, "tile", "grp", None),
            P(None, None, "tile", "grp", None),
            P(None, "tile", "grp", None),
            P(),
            P(),
            P(),
        ),
        out_specs=(P("grp", None, "tile", None), P(None, "tile", None)),
        check_vma=False,
    )
```

```python
import functools

import jax
import jax.numpy as jnp
import ml_dtypes
import numpy as np
from jax import lax
from jax.experimental import pallas as pl
from jax.experimental.pallas import tpu as pltpu
from jax.sharding import PartitionSpec as P

SECTION_WEIGHTS = (1.0 / 3.0, 0.5, 1.0)
TOGETHER = 3
SLOTS = 32
VMEM_LIMIT = 24 * 1024 * 1024


def pairs(count):
    near = [(i, i ^ 1) for i in range(count)]
    far = [(i, (i + (1 if i % 2 else -1)) % count) for i in range(count)]
    return near, far


def stencil_weights(width):
    out = np.zeros((2, 2 * width, 2 * width), np.float32)
    for side in range(2):
        for j in range(width):
            face = j + side
            for tap, value in enumerate((2.0, -13.0, 47.0, 27.0, -3.0)):
                up = min(max(face - 3 + tap, 0), width - 1)
                down = min(max(face + 2 - tap, 0), width - 1)
                for half in (0, width):
                    out[side, half + up, j] += value
                    out[side, half + down, width + j] += value
    return out.astype(ml_dtypes.bfloat16)


def advect_kernel(
    dims,
    table_ref,
    own_ref,
    near_ref,
    far_ref,
    met_own_ref,
    met_near_ref,
    met_far_ref,
    weights_ref,
    out_ref,
    mass_ref,
    q_a,
    q_b,
    q_c,
    q_d,
    start_ref,
    coef_ref,
):
    steps, levels, cells, block, groups, tracers, stride = dims
    width = 128
    rows = 3 * cells
    tiles = lax.axis_size("tile")
    here = lax.axis_index("tile")
    gains = steps * levels
    flips = gains + 2 * levels
    low_flip = table_ref[flips + lax.rem(here + tiles - 1, tiles)]
    high_flip = table_ref[flips + here]
    odd = lax.rem(here, 2) == 1

    lane = lax.broadcasted_iota(jnp.int32, (8, width), 1)
    row = lax.broadcasted_iota(jnp.int32, (8, width), 0)
    first_row = row == 0
    last_row = row == groups - 1

    def order_of(flip):
        return jnp.where(flip == 1.0, width - 1 - lane, lane)

    low_order = order_of(low_flip)
    high_order = order_of(high_flip)
    low_sign = jnp.where(low_flip == 1.0, -1.0, 1.0).astype(jnp.float32)
    high_sign = jnp.where(high_flip == 1.0, -1.0, 1.0).astype(jnp.float32)

    odd_mask = jnp.where(odd, lane, lane - width) >= 0

    def chosen(below, near, far):
        return jnp.where(odd_mask, near, far) if below else jnp.where(odd_mask, far, near)

    def turned(values, order):
        return jnp.take_along_axis(values, order, axis=1)

    def shift(values, by):
        return pltpu.roll(values, by % width, 1)

    def coefficients(level, slot):
        gain_a = table_ref[gains + level]
        gain_b = table_ref[gains + levels + level]

        def take(t, first):
            at = pl.ds(first, 8, stride=stride)
            if t == 1:
                return met_own_ref[at, :]
            return chosen(t == 0, met_near_ref[at, :], met_far_ref[at, :])

        orders = (low_order, None, high_order)
        signs = (low_sign, None, high_sign)
        mass = None
        for s in range(steps):
            flux_x = [[None] * block for _ in range(3)]
            flux_y = [[None] * block for _ in range(3)]
            start = [[None] * block for _ in range(3)]
            for t in range(3):
                for c in range(block):
                    at = s * levels * block + level * block + c
                    pressure = take(t, 112 + s * block + c)
                    met = gain_a + gain_b * pressure
                    x = take(t, at) * met
                    y = take(t, 56 + at) * met
                    if orders[t] is not None:
                        x = turned(x, orders[t])
                        y = turned(y, orders[t]) * signs[t]
                        if s == 0:
                            met = turned(met, orders[t])
                    flux_x[t][c] = x
                    flux_y[t][c] = y
                    start[t][c] = met
            if s == 0:
                mass = start
            face_x = [[None] * block for _ in range(3)]
            for t in range(3):
                for c in range(block):
                    if c:
                        before = flux_x[t][c - 1]
                    else:
                        before = pltpu.roll(flux_x[t][block - 1], 1, 0)
                        if t:
                            before = jnp.where(first_row, pltpu.roll(flux_x[t - 1][block - 1], 1, 0), before)
                    face_x[t][c] = 0.5 * (before + flux_x[t][c])
            for t in range(3):
                for c in range(block):
                    if c < block - 1:
                        after = face_x[t][c + 1]
                    else:
                        after = pltpu.roll(face_x[t][0], groups - 1, 0)
                        if t < 2:
                            after = jnp.where(last_row, pltpu.roll(face_x[t + 1][0], groups - 1, 0), after)
                    face_y = jnp.where(lane == 0, 0.0, 0.5 * (shift(flux_y[t][c], 1) + flux_y[t][c]))
                    next_y = shift(face_y, -1)
                    div = (after - face_x[t][c]) + (next_y - face_y)
                    kinds = [jnp.abs(face_x[t][c]) * (1.0 / 30.0), face_y * (1.0 / 60.0), next_y * (1.0 / 60.0)]
                    for weight in SECTION_WEIGHTS:
                        kinds.append(weight / (mass[t][c] - weight * div))
                    kinds.append(mass[t][c])
                    for kind, value in enumerate(kinds):
                        coef_ref[slot, s, pl.ds((t * cells + c) * 8 + kind, 8, stride=8 * block), :] = value
                    mass[t][c] = mass[t][c] - div
        for c in range(block):
            mass_ref[pl.ds(level * cells + c, 8, stride=block), :] = mass[1][c]

    def run(*accs):
        for side in range(2):
            pltpu.matmul_push_rhs(weights_ref[side], 0, side)
        for side in range(2):
            pltpu.matmul_acc_lhs(accs[side], jnp.zeros((16, 256), jnp.bfloat16), load_staged_rhs=0)
            out_ref[0:16, :] = pltpu.matmul_pop(accs[side])[:, :width]

        def group_body(group, carry):
            flow = []
            for slot in range(TOGETHER):
                level = group * TOGETHER + slot
                coefficients(level, slot)
                ahead = [table_ref[s * levels + level] > 0.0 for s in range(steps)]
                way = [jnp.where(a, 1, -1).astype(jnp.int32) for a in ahead]
                same = way[0] == way[1]
                first = jnp.where(same, cells - 9, cells - 6)
                inlet = [first - 6, jnp.int32(cells - 6)]
                base = [jnp.where(a, p, rows - 1 - p) for a, p in zip(ahead, inlet)]
                for r in range(6, rows - 6):
                    if r < cells:
                        at = pl.ds(pl.multiple_of((level * 18 + r - 6) * tracers, 8), tracers)
                        value = turned(chosen(True, near_ref[at, :], far_ref[at, :]), low_order)
                    elif r < 2 * cells:
                        value = own_ref[pl.ds(level * cells + r - cells, tracers, stride=levels * cells), :]
                    else:
                        at = pl.ds(pl.multiple_of((level * 18 + r - 2 * cells) * tracers, 8), tracers)
                        value = turned(chosen(False, near_ref[at, :], far_ref[at, :]), high_order)
                    q_a[slot, (r - base[0]) * way[0] + 6] = value
                flow.append((level, ahead, way, same, base))

            plan = [
                (0, 0, q_a, 3, q_b),
                (0, 1, q_b, 0, q_c),
                (0, 2, q_c, 0, q_d),
                (1, 0, q_d, 0, q_b),
                (1, 1, q_b, 0, q_c),
                (1, 2, q_c, 0, None),
            ]
            items = [(n, slot) for n in range(6) for slot in range(TOGETHER)]
            counts = [cells + 5 * (5 - n) for n in range(6)]
            parts = [-(-c // 2) for c in counts]
            pushed, popped = [0], [0]

            def push(item, part):
                n, slot = item
                _, _, source, pad, _ = plan[n]
                at = 2 * part + 3 + pad
                both = jnp.concatenate([source[slot, at], source[slot, at + 1]], axis=0)
                high = both.astype(jnp.bfloat16)
                rest = (both - high.astype(jnp.float32)).astype(jnp.bfloat16)
                lhs = jnp.concatenate([high, rest], axis=1)
                place = pushed[0] % SLOTS
                pushed[0] += 1
                for side in range(2):
                    pltpu.matmul_acc_lhs(accs[2 * place + side], lhs)

            state = {}

            def finish(item, part):
                n, slot = item
                s, number, source, pad, target = plan[n]
                level, ahead, way, same, base = flow[slot]
                weight = SECTION_WEIGHTS[number]
                place = popped[0] % SLOTS
                popped[0] += 1
                pops = [pltpu.matmul_pop(accs[2 * place + side]) for side in range(2)]
                if part == 0:
                    state.clear()

                def spot(k):
                    return base[s] + way[s] * (k + 3 * number)

                def spread(at, kind):
                    return jnp.broadcast_to(coef_ref[slot, s, pl.ds(at * 8 + kind, 1), :], (8, width))

                def q(k):
                    if k not in state:
                        state[k] = source[slot, k + pad]
                    return state[k]

                def along_x(k):
                    at = spot(k) + jnp.where(ahead[s], 0, 1)
                    five = ((q(k) - 6.5 * q(k + 1)) + (23.5 * q(k + 2) + 13.5 * q(k + 3))) - 1.5 * q(k + 4)
                    return spread(at, 0) * five

                if part == 0:
                    state["before"] = along_x(0)
                for half in range(2):
                    k = 2 * part + half
                    if k >= counts[n]:
                        continue
                    at = spot(k)
                    after = along_x(k + 1)
                    sides = []
                    for side in range(2):
                        flux = spread(at, 1 + side)
                        rows_of = pops[side][8 * half : 8 * half + 8]
                        sides.append(flux * jnp.where(flux >= 0.0, rows_of[:, :width], rows_of[:, width:]))
                    div = (after - state["before"]) + (sides[1] - sides[0])
                    if number == 0:
                        start = q(k + 3) * spread(at, 6)
                        start_ref[slot, k] = start
                    else:
                        start = start_ref[slot, k + 3 * number]
                    if weight != 1.0:
                        start = start * (1.0 / weight)
                    value = (start - div) * spread(at, 3 + number)
                    if target is None:
                        i = jnp.where(ahead[1], k, cells - 1 - k)
                        out_ref[pl.ds(level * cells + i, tracers, stride=levels * cells), :] = value
                    elif target is q_d:
                        q_d[slot, jnp.where(same, k, counts[n] - 1 - k)] = value
                    else:
                        target[slot, k] = value
                    state["before"] = after
                    state.pop(k, None)

            for part in range(parts[0]):
                push(items[0], part)
            for index, item in enumerate(items):
                following = items[index + 1] if index + 1 < len(items) else None
                ahead_parts = parts[following[0]] if following else 0
                for part in range(max(parts[item[0]], ahead_parts)):
                    if part < parts[item[0]]:
                        finish(item, part)
                    if part < ahead_parts:
                        push(following, part)
            return carry

        lax.fori_loop(0, levels // TOGETHER, group_body, 0)

    acc = [pltpu.ACC(side)((16, 256), jnp.float32) for _ in range(SLOTS) for side in range(2)]
    pl.run_scoped(run, *acc)


def edge_kernel(levels, cells, tracers, field_ref, near_ref, far_ref):
    even = lax.rem(lax.axis_index("tile"), 2) == 0
    near_row = jnp.where(even, cells - 18, 0)
    far_row = cells - 18 - near_row

    def level_body(level, carry):
        for r in range(18):
            at = pl.ds(pl.multiple_of((level * 18 + r) * tracers, 8), tracers)
            for ref, row in ((near_ref, near_row), (far_ref, far_row)):
                ref[at, :] = field_ref[pl.ds(level * cells + row + r, tracers, stride=levels * cells), :]
        return carry

    lax.fori_loop(0, levels, level_body, 0)


def met_kernel(groups, x_ref, y_ref, p_ref, out_ref):
    for ref, first in ((x_ref, 0), (y_ref, 56), (p_ref, 112)):
        count = ref.shape[0]
        value = ref[...].reshape(count, ref.shape[2])
        for g in range(groups):
            out_ref[g, first : first + count, :] = value


def local(tracers, wind_x, wind_y, surface_p, coef_a, coef_b, edge_flip):
    count, levels, cells, width = tracers.shape
    steps, block = wind_x.shape[0], wind_x.shape[3]
    groups, tiles = lax.axis_size("grp"), lax.axis_size("tile")
    stride = 120
    smem = pl.BlockSpec(memory_space=pltpu.SMEM)
    vmem = pl.BlockSpec(memory_space=pltpu.VMEM)
    flat = (count * levels * cells, width)
    edge = jax.ShapeDtypeStruct((levels * 18 * count, width), jnp.float32)

    near_pairs, far_pairs = pairs(tiles)
    table = jnp.concatenate(
        [wind_x[:, :, 0, 0, 0].reshape(-1), coef_a, coef_b, edge_flip.astype(jnp.float32)], axis=0
    )
    near, far = pl.pallas_call(
        functools.partial(edge_kernel, levels, cells, count),
        out_shape=(edge, edge),
        in_specs=[vmem],
        out_specs=(vmem, vmem),
        name="edges",
    )(tracers.reshape(flat))
    near = lax.ppermute(near, "tile", near_pairs)
    far = lax.ppermute(far, "tile", far_pairs)
    packed = pl.pallas_call(
        functools.partial(met_kernel, groups),
        out_shape=jax.ShapeDtypeStruct((groups, stride, width), jnp.float32),
        in_specs=[vmem] * 3,
        out_specs=vmem,
        name="met",
    )(wind_x.reshape(-1, 1, width), wind_y.reshape(-1, 1, width), surface_p.reshape(-1, 1, width))
    met = lax.all_to_all(packed, "grp", 0, 0, tiled=True)
    met_near = lax.ppermute(met, "tile", near_pairs)
    met_far = lax.ppermute(met, "tile", far_pairs)

    met_flat = (groups * stride, width)
    dims = (steps, levels, cells, block, groups, count, stride)
    rows = 3 * cells
    out, mass = pl.pallas_call(
        functools.partial(advect_kernel, dims),
        out_shape=(
            jax.ShapeDtypeStruct(flat, jnp.float32),
            jax.ShapeDtypeStruct((levels * cells, width), jnp.float32),
        ),
        in_specs=[smem] + [vmem] * 7,
        out_specs=(vmem, vmem),
        scratch_shapes=[
            pltpu.VMEM((TOGETHER, 64, count, width), jnp.float32),
            pltpu.VMEM((TOGETHER, 56, count, width), jnp.float32),
            pltpu.VMEM((TOGETHER, 56, count, width), jnp.float32),
            pltpu.VMEM((TOGETHER, 40, count, width), jnp.float32),
            pltpu.VMEM((TOGETHER, 56, count, width), jnp.float32),
            pltpu.VMEM((TOGETHER, steps, rows * 8, width), jnp.float32),
        ],
        compiler_params=pltpu.CompilerParams(vmem_limit_bytes=VMEM_LIMIT),
        name="advect",
    )(
        table,
        tracers.reshape(flat),
        near,
        far,
        met.reshape(met_flat),
        met_near.reshape(met_flat),
        met_far.reshape(met_flat),
        jnp.asarray(stencil_weights(width)),
    )
    return out.reshape(tracers.shape), mass.reshape(levels, cells, width)


def solution(mesh):
    return jax.shard_map(
        local,
        mesh=mesh,
        in_specs=(
            P("grp", None, "tile", None),
            P(None, None, "tile", "grp", None),
            P(None, None, "tile", "grp", None),
            P(None, "tile", "grp", None),
            P(),
            P(),
            P(),
        ),
        out_specs=(P("grp", None, "tile", None), P(None, "tile", None)),
        check_vma=False,
    )
```

```python
import functools

import jax
import jax.numpy as jnp
import ml_dtypes
import numpy as np
from jax import lax
from jax.experimental import pallas as pl
from jax.experimental.pallas import tpu as pltpu
from jax.sharding import PartitionSpec as P

SECTION_WEIGHTS = (1.0 / 3.0, 0.5, 1.0)
TOGETHER = 3
ROWS = 64
KINDS = 7
SLOTS = 32
VMEM_LIMIT = 24 * 1024 * 1024


def pairs(count):
    near = [(i, i ^ 1) for i in range(count)]
    far = [(i, (i + (1 if i % 2 else -1)) % count) for i in range(count)]
    return near, far


def stencil_weights(width):
    out = np.zeros((2, 2 * width, 2 * width), np.float32)
    for side in range(2):
        for j in range(width):
            face = j + side
            for tap, value in enumerate((2.0, -13.0, 47.0, 27.0, -3.0)):
                up = min(max(face - 3 + tap, 0), width - 1)
                down = min(max(face + 2 - tap, 0), width - 1)
                for half in (0, width):
                    out[side, half + up, j] += value
                    out[side, half + down, width + j] += value
    return out.astype(ml_dtypes.bfloat16)


def advect_kernel(
    dims,
    table_ref,
    own_ref,
    near_ref,
    far_ref,
    met_own_ref,
    met_near_ref,
    met_far_ref,
    weights_hbm,
    out_ref,
    mass_ref,
    q_a,
    q_b,
    q_c,
    q_d,
    start_ref,
    coef_ref,
    met_side_ref,
    weights_ref,
    weights_sem,
):
    steps, levels, cells, block, groups, tracers, stride = dims
    width = 128
    rows = 3 * cells
    tiles = lax.axis_size("tile")
    here = lax.axis_index("tile")
    gains = steps * levels
    flips = gains + 2 * levels
    low_flip = table_ref[flips + lax.rem(here + tiles - 1, tiles)]
    high_flip = table_ref[flips + here]
    odd = lax.rem(here, 2) == 1

    lane = lax.broadcasted_iota(jnp.int32, (8, width), 1)
    row = lax.broadcasted_iota(jnp.int32, (8, width), 0)
    first_row = row == 0
    last_row = row == groups - 1

    def order_of(flip):
        return jnp.where(flip == 1.0, width - 1 - lane, lane)

    def neighbour_orders(flip):
        flipped = flip == 1.0
        order = order_of(flip)
        before = jnp.where(flipped, jnp.minimum(order + 1, width - 1), jnp.maximum(order - 1, 0))
        after = jnp.where(flipped, jnp.maximum(order - 1, 0), jnp.minimum(order + 1, width - 1))
        return order, before, after

    low_orders = neighbour_orders(low_flip)
    high_orders = neighbour_orders(high_flip)
    low_order, high_order = low_orders[0], high_orders[0]
    low_sign = jnp.where(low_flip == 1.0, -1.0, 1.0).astype(jnp.float32)
    high_sign = jnp.where(high_flip == 1.0, -1.0, 1.0).astype(jnp.float32)

    odd_mask = jnp.where(odd, lane, lane - width) >= 0

    def chosen(below, near, far):
        return jnp.where(odd_mask, near, far) if below else jnp.where(odd_mask, far, near)

    def turned(values, order):
        return jnp.take_along_axis(values, order, axis=1)

    def shift(values, by):
        return pltpu.roll(values, by % width, 1)

    def coefficients(level, slot):
        gain_a = table_ref[gains + level]
        gain_b = table_ref[gains + levels + level]

        def take(t, s, first):
            if t == 1:
                return met_own_ref[pl.ds(s * ROWS + first, 8, stride=stride), :]
            return met_side_ref[t // 2, pl.ds((0 if (t == 0) == (s == 0) else 3) * ROWS + first, 8, stride=ROWS), :]

        orders = (low_orders, None, high_orders)
        signs = (low_sign, None, high_sign)
        mass = None
        for s in range(steps):
            flux_x = [[None] * block for _ in range(3)]
            faces_y = [[None] * block for _ in range(3)]
            start = [[None] * block for _ in range(3)]
            for t in range(3):
                for c in range(block):
                    at = level * block + c
                    pressure = take(t, s, 2 * levels * block + c)
                    met = gain_a + gain_b * pressure
                    x = take(t, s, at) * met
                    y = take(t, s, levels * block + at) * met
                    if orders[t] is not None:
                        order, order_before, order_after = orders[t]
                        x = turned(x, order)
                        y = y * signs[t]
                        y_before, y_after, y = turned(y, order_before), turned(y, order_after), turned(y, order)
                        if s == 0:
                            met = turned(met, order)
                    else:
                        y_before, y_after = shift(y, 1), shift(y, -1)
                    flux_x[t][c] = x
                    faces_y[t][c] = (
                        jnp.where(lane == 0, 0.0, 0.5 * (y_before + y)),
                        jnp.where(lane == width - 1, 0.0, 0.5 * (y + y_after)),
                    )
                    start[t][c] = met
            if s == 0:
                mass = start
            face_x = [[None] * block for _ in range(3)]
            for t in range(3):
                for c in range(block):
                    if c:
                        before = flux_x[t][c - 1]
                    else:
                        before = pltpu.roll(flux_x[t][block - 1], 1, 0)
                        if t:
                            before = jnp.where(first_row, pltpu.roll(flux_x[t - 1][block - 1], 1, 0), before)
                    face_x[t][c] = 0.5 * (before + flux_x[t][c])
            for t in range(3):
                for c in range(block):
                    if c < block - 1:
                        after = face_x[t][c + 1]
                    else:
                        after = pltpu.roll(face_x[t][0], groups - 1, 0)
                        if t < 2:
                            after = jnp.where(last_row, pltpu.roll(face_x[t + 1][0], groups - 1, 0), after)
                    face_y, next_y = faces_y[t][c]
                    div = (after - face_x[t][c]) + (next_y - face_y)
                    kinds = [jnp.abs(face_x[t][c]) * (1.0 / 30.0), face_y * (1.0 / 60.0), next_y * (1.0 / 60.0)]
                    for weight in SECTION_WEIGHTS:
                        kinds.append(weight / (mass[t][c] - weight * div))
                    kinds.append(mass[t][c])
                    for kind, value in enumerate(kinds):
                        coef_ref[slot, s, pl.ds((t * cells + c) * KINDS + kind, 8, stride=KINDS * block), :] = value
                    mass[t][c] = mass[t][c] - div
        for c in range(block):
            mass_ref[pl.ds(level * cells + c, 8, stride=block), :] = mass[1][c]

    def run(*accs):
        fetch = pltpu.make_async_copy(weights_hbm, weights_ref, weights_sem)
        fetch.start()
        met_side_ref[0, 0 : 2 * ROWS, :] = jnp.zeros((2 * ROWS, width), jnp.float32)
        met_side_ref[1, 9 * ROWS : 11 * ROWS, :] = jnp.zeros((2 * ROWS, width), jnp.float32)
        for r in range(0, 9 * ROWS, 8):
            near, far = met_near_ref[r : r + 8, :], met_far_ref[r : r + 8, :]
            met_side_ref[0, 2 * ROWS + r : 2 * ROWS + r + 8, :] = chosen(True, near, far)
            met_side_ref[1, r : r + 8, :] = chosen(False, near, far)
        for level in range(levels):
            coefficients(level, level)

        fetch.wait()
        for side in range(2):
            pltpu.matmul_push_rhs(weights_ref[side], 0, side)
        for side in range(2):
            pltpu.matmul_acc_lhs(accs[side], jnp.zeros((16, 256), jnp.bfloat16), load_staged_rhs=0)
            out_ref[0:16, :] = pltpu.matmul_pop(accs[side])[:, :width]

        def group_body(group, carry):
            flow = []
            for slot in range(TOGETHER):
                level = group * TOGETHER + slot
                ahead = [table_ref[s * levels + level] > 0.0 for s in range(steps)]
                way = [jnp.where(a, 1, -1).astype(jnp.int32) for a in ahead]
                same = way[0] == way[1]
                first = jnp.where(same, cells - 9, cells - 6)
                inlet = [first - 6, jnp.int32(cells - 6)]
                base = [jnp.where(a, p, rows - 1 - p) for a, p in zip(ahead, inlet)]
                for r in range(6, rows - 6):
                    if r < cells:
                        at = pl.ds(pl.multiple_of((level * 18 + r - 6) * tracers, 8), tracers)
                        value = turned(chosen(True, near_ref[at, :], far_ref[at, :]), low_order)
                    elif r < 2 * cells:
                        value = own_ref[pl.ds(level * cells + r - cells, tracers, stride=levels * cells), :]
                    else:
                        at = pl.ds(pl.multiple_of((level * 18 + r - 2 * cells) * tracers, 8), tracers)
                        value = turned(chosen(False, near_ref[at, :], far_ref[at, :]), high_order)
                    q_a[slot, (r - base[0]) * way[0] + 6] = value
                flow.append((level, ahead, way, same, base))

            plan = [
                (0, 0, q_a, 3, q_b),
                (0, 1, q_b, 0, q_c),
                (0, 2, q_c, 0, q_d),
                (1, 0, q_d, 0, q_b),
                (1, 1, q_b, 0, q_c),
                (1, 2, q_c, 0, None),
            ]
            items = [(n, slot) for n in range(6) for slot in range(TOGETHER)]
            counts = [cells + 5 * (5 - n) for n in range(6)]
            parts = [-(-c // 2) for c in counts]
            pushed, popped = [0], [0]

            def push(item, part):
                n, slot = item
                _, _, source, pad, _ = plan[n]
                at = 2 * part + 3 + pad
                both = jnp.concatenate([source[slot, at], source[slot, at + 1]], axis=0)
                high = both.astype(jnp.bfloat16)
                rest = (both - high.astype(jnp.float32)).astype(jnp.bfloat16)
                lhs = jnp.concatenate([high, rest], axis=1)
                place = pushed[0] % SLOTS
                pushed[0] += 1
                for side in range(2):
                    pltpu.matmul_acc_lhs(accs[2 * place + side], lhs)

            state = {}

            def finish(item, part):
                n, slot = item
                s, number, source, pad, target = plan[n]
                level, ahead, way, same, base = flow[slot]
                weight = SECTION_WEIGHTS[number]
                place = popped[0] % SLOTS
                popped[0] += 1
                pops = [pltpu.matmul_pop(accs[2 * place + side]) for side in range(2)]
                if part == 0:
                    state.clear()

                def spot(k):
                    return base[s] + way[s] * (k + 3 * number)

                def spread(at, kind):
                    return jnp.broadcast_to(coef_ref[level, s, pl.ds(at * KINDS + kind, 1), :], (8, width))

                def q(k):
                    if k not in state:
                        state[k] = source[slot, k + pad]
                    return state[k]

                def along_x(k):
                    at = spot(k) + jnp.where(ahead[s], 0, 1)
                    five = ((q(k) - 6.5 * q(k + 1)) + (23.5 * q(k + 2) + 13.5 * q(k + 3))) - 1.5 * q(k + 4)
                    return spread(at, 0) * five

                if part == 0:
                    state["before"] = along_x(0)
                for half in range(2):
                    k = 2 * part + half
                    if k >= counts[n]:
                        continue
                    at = spot(k)
                    after = along_x(k + 1)
                    sides = []
                    for side in range(2):
                        flux = spread(at, 1 + side)
                        rows_of = pops[side][8 * half : 8 * half + 8]
                        sides.append(flux * jnp.where(flux >= 0.0, rows_of[:, :width], rows_of[:, width:]))
                    div = (after - state["before"]) + (sides[1] - sides[0])
                    if number == 0:
                        start = q(k + 3) * spread(at, 6)
                        start_ref[slot, k] = start
                    else:
                        start = start_ref[slot, k + 3 * number]
                    if weight != 1.0:
                        start = start * (1.0 / weight)
                    value = (start - div) * spread(at, 3 + number)
                    if target is None:
                        i = jnp.where(ahead[1], k, cells - 1 - k)
                        out_ref[pl.ds(level * cells + i, tracers, stride=levels * cells), :] = value
                    elif target is q_d:
                        q_d[slot, jnp.where(same, k, counts[n] - 1 - k)] = value
                    else:
                        target[slot, k] = value
                    state["before"] = after
                    state.pop(k, None)

            for part in range(parts[0]):
                push(items[0], part)
            for index, item in enumerate(items):
                following = items[index + 1] if index + 1 < len(items) else None
                ahead_parts = parts[following[0]] if following else 0
                for part in range(max(parts[item[0]], ahead_parts)):
                    if part < parts[item[0]]:
                        finish(item, part)
                    if part < ahead_parts:
                        push(following, part)
            return carry

        lax.fori_loop(0, levels // TOGETHER, group_body, 0)

    acc = [pltpu.ACC(side)((16, 256), jnp.float32) for _ in range(SLOTS) for side in range(2)]
    pl.run_scoped(run, *acc)


def edge_kernel(levels, cells, tracers, field_ref, near_ref, far_ref):
    even = lax.rem(lax.axis_index("tile"), 2) == 0
    near_row = jnp.where(even, cells - 18, 0)
    far_row = cells - 18 - near_row

    def level_body(level, carry):
        for r in range(18):
            at = pl.ds(pl.multiple_of((level * 18 + r) * tracers, 8), tracers)
            for ref, row in ((near_ref, near_row), (far_ref, far_row)):
                ref[at, :] = field_ref[pl.ds(level * cells + row + r, tracers, stride=levels * cells), :]
        return carry

    lax.fori_loop(0, levels, level_body, 0)


def met_kernel(groups, steps, x_ref, y_ref, p_ref, out_ref):
    for s in range(steps):
        first = s * ROWS
        for ref in (x_ref, y_ref, p_ref):
            count = ref.shape[0] // steps
            value = ref[s * count : (s + 1) * count].reshape(count, ref.shape[2])
            for g in range(groups):
                out_ref[g, first : first + count, :] = value
            first += count


def block_kernel(met_ref, near_ref, far_ref):
    odd = lax.rem(lax.axis_index("tile"), 2) == 1

    def fill(above_ref, below_ref):
        for slot, (s, g) in enumerate([(0, g) for g in range(2, 8)] + [(1, 5), (1, 6), (1, 7)]):
            above_ref[slot * ROWS : (slot + 1) * ROWS, :] = met_ref[g, s * ROWS : (s + 1) * ROWS, :]
        for slot, (s, g) in enumerate([(1, 0), (1, 1), (1, 2)] + [(0, g) for g in range(6)]):
            below_ref[slot * ROWS : (slot + 1) * ROWS, :] = met_ref[g, s * ROWS : (s + 1) * ROWS, :]

    @pl.when(odd)
    def _():
        fill(far_ref, near_ref)

    @pl.when(jnp.logical_not(odd))
    def _():
        fill(near_ref, far_ref)


def local(tracers, wind_x, wind_y, surface_p, coef_a, coef_b, edge_flip):
    count, levels, cells, width = tracers.shape
    steps, block = wind_x.shape[0], wind_x.shape[3]
    groups, tiles = lax.axis_size("grp"), lax.axis_size("tile")
    stride = steps * ROWS
    smem = pl.BlockSpec(memory_space=pltpu.SMEM)
    vmem = pl.BlockSpec(memory_space=pltpu.VMEM)
    flat = (count * levels * cells, width)
    small = pltpu.CompilerParams(vmem_limit_bytes=8 * 1024 * 1024)
    edge = jax.ShapeDtypeStruct((levels * 18 * count, width), jnp.float32)

    near_pairs, far_pairs = pairs(tiles)
    table = jnp.concatenate(
        [wind_x[:, :, 0, 0, 0].reshape(-1), coef_a, coef_b, edge_flip.astype(jnp.float32)], axis=0
    )
    near, far = pl.pallas_call(
        functools.partial(edge_kernel, levels, cells, count),
        out_shape=(edge, edge),
        in_specs=[vmem],
        out_specs=(vmem, vmem),
        name="edges",
    )(tracers.reshape(flat))
    near = lax.ppermute(near, "tile", near_pairs)
    far = lax.ppermute(far, "tile", far_pairs)
    packed = pl.pallas_call(
        functools.partial(met_kernel, groups, steps),
        out_shape=jax.ShapeDtypeStruct((groups, stride, width), jnp.float32),
        in_specs=[vmem] * 3,
        out_specs=vmem,
        name="met",
    )(wind_x.reshape(-1, 1, width), wind_y.reshape(-1, 1, width), surface_p.reshape(-1, 1, width))
    met = lax.all_to_all(packed, "grp", 0, 0, tiled=True)
    part = jax.ShapeDtypeStruct((9 * ROWS, width), jnp.float32)
    met_near, met_far = pl.pallas_call(
        block_kernel, out_shape=(part, part), in_specs=[vmem], out_specs=(vmem, vmem), compiler_params=small, name="blocks"
    )(met)
    met_near = lax.ppermute(met_near, "tile", near_pairs)
    met_far = lax.ppermute(met_far, "tile", far_pairs)

    met_flat = (groups * stride, width)
    dims = (steps, levels, cells, block, groups, count, stride)
    rows = 3 * cells
    out, mass = pl.pallas_call(
        functools.partial(advect_kernel, dims),
        out_shape=(
            jax.ShapeDtypeStruct(flat, jnp.float32),
            jax.ShapeDtypeStruct((levels * cells, width), jnp.float32),
        ),
        in_specs=[smem] + [vmem] * 6 + [pl.BlockSpec(memory_space=pl.ANY)],
        out_specs=(vmem, vmem),
        scratch_shapes=[
            pltpu.VMEM((TOGETHER, 64, count, width), jnp.float32),
            pltpu.VMEM((TOGETHER, 56, count, width), jnp.float32),
            pltpu.VMEM((TOGETHER, 56, count, width), jnp.float32),
            pltpu.VMEM((TOGETHER, 40, count, width), jnp.float32),
            pltpu.VMEM((TOGETHER, 56, count, width), jnp.float32),
            pltpu.VMEM((levels, steps, rows * KINDS, width), jnp.float32),
            pltpu.VMEM((2, 11 * ROWS, width), jnp.float32),
            pltpu.VMEM((2, 2 * width, 2 * width), jnp.bfloat16),
            pltpu.SemaphoreType.DMA,
        ],
        compiler_params=pltpu.CompilerParams(vmem_limit_bytes=VMEM_LIMIT),
        name="advect",
    )(
        table,
        tracers.reshape(flat),
        near,
        far,
        met.reshape(met_flat),
        met_near,
        met_far,
        jnp.asarray(stencil_weights(width)),
    )
    return out.reshape(tracers.shape), mass.reshape(levels, cells, width)


def solution(mesh):
    return jax.shard_map(
        local,
        mesh=mesh,
        in_specs=(
            P("grp", None, "tile", None),
            P(None, None, "tile", "grp", None),
            P(None, None, "tile", "grp", None),
            P(None, "tile", "grp", None),
            P(),
            P(),
            P(),
        ),
        out_specs=(P("grp", None, "tile", None), P(None, "tile", None)),
        check_vma=False,
    )
```

```python
import functools

import jax
import jax.numpy as jnp
import ml_dtypes
import numpy as np
from jax import lax
from jax.experimental import pallas as pl
from jax.experimental.pallas import tpu as pltpu
from jax.sharding import PartitionSpec as P

SECTION_WEIGHTS = (1.0 / 3.0, 0.5, 1.0)
TOGETHER = 3
ROWS = 64
KINDS = 7
SLOTS = 32
VMEM_LIMIT = 24 * 1024 * 1024


def pairs(count):
    near = [(i, i ^ 1) for i in range(count)]
    far = [(i, (i + (1 if i % 2 else -1)) % count) for i in range(count)]
    return near, far


def stencil_weights(width):
    out = np.zeros((2, 2 * width, 2 * width), np.float32)
    for side in range(2):
        for j in range(width):
            face = j + side
            for tap, value in enumerate((2.0, -13.0, 47.0, 27.0, -3.0)):
                up = min(max(face - 3 + tap, 0), width - 1)
                down = min(max(face + 2 - tap, 0), width - 1)
                for half in (0, width):
                    out[side, half + up, j] += value
                    out[side, half + down, width + j] += value
    return out.astype(ml_dtypes.bfloat16)


def advect_kernel(
    dims,
    table_ref,
    own_ref,
    near_ref,
    far_ref,
    met_own_ref,
    met_near_ref,
    met_far_ref,
    weights_hbm,
    out_ref,
    mass_ref,
    q_a,
    q_b,
    q_c,
    q_d,
    start_ref,
    coef_ref,
    met_side_ref,
    weights_ref,
    weights_sem,
):
    steps, levels, cells, block, groups, tracers, stride = dims
    width = 128
    rows = 3 * cells
    tiles = lax.axis_size("tile")
    here = lax.axis_index("tile")
    gains = steps * levels
    flips = gains + 2 * levels
    low_flip = table_ref[flips + lax.rem(here + tiles - 1, tiles)]
    high_flip = table_ref[flips + here]
    odd = lax.rem(here, 2) == 1

    lane = lax.broadcasted_iota(jnp.int32, (8, width), 1)
    row = lax.broadcasted_iota(jnp.int32, (8, width), 0)
    first_row = row == 0
    last_row = row == groups - 1

    def order_of(flip):
        return jnp.where(flip == 1.0, width - 1 - lane, lane)

    def neighbour_orders(flip):
        flipped = flip == 1.0
        order = order_of(flip)
        before = jnp.where(flipped, jnp.minimum(order + 1, width - 1), jnp.maximum(order - 1, 0))
        after = jnp.where(flipped, jnp.maximum(order - 1, 0), jnp.minimum(order + 1, width - 1))
        return order, before, after

    low_orders = neighbour_orders(low_flip)
    high_orders = neighbour_orders(high_flip)
    low_order, high_order = low_orders[0], high_orders[0]
    low_sign = jnp.where(low_flip == 1.0, -1.0, 1.0).astype(jnp.float32)
    high_sign = jnp.where(high_flip == 1.0, -1.0, 1.0).astype(jnp.float32)

    odd_mask = jnp.where(odd, lane, lane - width) >= 0

    def chosen(below, near, far):
        return jnp.where(odd_mask, near, far) if below else jnp.where(odd_mask, far, near)

    def turned(values, order):
        return jnp.take_along_axis(values, order, axis=1)

    def shift(values, by):
        return pltpu.roll(values, by % width, 1)

    def coefficients(level, slot):
        gain_a = table_ref[gains + level]
        gain_b = table_ref[gains + levels + level]

        def take(t, s, first):
            if t == 1:
                return met_own_ref[pl.ds(s * ROWS + first, 8, stride=stride), :]
            return met_side_ref[t // 2, pl.ds((0 if (t == 0) == (s == 0) else 3) * ROWS + first, 8, stride=ROWS), :]

        orders = (low_orders, None, high_orders)
        signs = (low_sign, None, high_sign)
        mass = None
        for s in range(steps):
            flux_x = [[None] * block for _ in range(3)]
            faces_y = [[None] * block for _ in range(3)]
            start = [[None] * block for _ in range(3)]
            for t in range(3):
                for c in range(block):
                    at = level * block + c
                    pressure = take(t, s, 2 * levels * block + c)
                    met = gain_a + gain_b * pressure
                    x = take(t, s, at) * met
                    y = take(t, s, levels * block + at) * met
                    if orders[t] is not None:
                        order, order_before, order_after = orders[t]
                        x = turned(x, order)
                        y = y * signs[t]
                        y_before, y_after, y = turned(y, order_before), turned(y, order_after), turned(y, order)
                        if s == 0:
                            met = turned(met, order)
                    else:
                        y_before, y_after = shift(y, 1), shift(y, -1)
                    flux_x[t][c] = x
                    faces_y[t][c] = (
                        jnp.where(lane == 0, 0.0, 0.5 * (y_before + y)),
                        jnp.where(lane == width - 1, 0.0, 0.5 * (y + y_after)),
                    )
                    start[t][c] = met
            if s == 0:
                mass = start
            face_x = [[None] * block for _ in range(3)]
            for t in range(3):
                for c in range(block):
                    if c:
                        before = flux_x[t][c - 1]
                    else:
                        before = pltpu.roll(flux_x[t][block - 1], 1, 0)
                        if t:
                            before = jnp.where(first_row, pltpu.roll(flux_x[t - 1][block - 1], 1, 0), before)
                    face_x[t][c] = 0.5 * (before + flux_x[t][c])
            for t in range(3):
                for c in range(block):
                    if c < block - 1:
                        after = face_x[t][c + 1]
                    else:
                        after = pltpu.roll(face_x[t][0], groups - 1, 0)
                        if t < 2:
                            after = jnp.where(last_row, pltpu.roll(face_x[t + 1][0], groups - 1, 0), after)
                    face_y, next_y = faces_y[t][c]
                    div = (after - face_x[t][c]) + (next_y - face_y)
                    kinds = [jnp.abs(face_x[t][c]) * (1.0 / 30.0), face_y * (1.0 / 60.0), next_y * (1.0 / 60.0)]
                    for weight in SECTION_WEIGHTS:
                        kinds.append(weight / (mass[t][c] - weight * div))
                    kinds.append(mass[t][c])
                    for kind, value in enumerate(kinds):
                        coef_ref[slot, s, pl.ds((t * cells + c) * KINDS + kind, 8, stride=KINDS * block), :] = value
                    mass[t][c] = mass[t][c] - div
        for c in range(block):
            mass_ref[pl.ds(level * cells + c, 8, stride=block), :] = mass[1][c]

    def run(*accs):
        fetch = pltpu.make_async_copy(weights_hbm, weights_ref, weights_sem)
        fetch.start()
        met_side_ref[0, 0 : 2 * ROWS, :] = jnp.zeros((2 * ROWS, width), jnp.float32)
        met_side_ref[1, 9 * ROWS : 11 * ROWS, :] = jnp.zeros((2 * ROWS, width), jnp.float32)
        for r in range(0, 9 * ROWS, 8):
            near, far = met_near_ref[r : r + 8, :], met_far_ref[r : r + 8, :]
            met_side_ref[0, 2 * ROWS + r : 2 * ROWS + r + 8, :] = chosen(True, near, far)
            met_side_ref[1, r : r + 8, :] = chosen(False, near, far)
        for level in range(levels):
            coefficients(level, level)

        fetch.wait()
        for side in range(2):
            pltpu.matmul_push_rhs(weights_ref[side], 0, side)
        for side in range(2):
            pltpu.matmul_acc_lhs(accs[side], jnp.zeros((16, 256), jnp.bfloat16), load_staged_rhs=0)
            out_ref[0:16, :] = pltpu.matmul_pop(accs[side])[:, :width]

        def group_body(group, carry):
            flow = []
            for slot in range(TOGETHER):
                level = group * TOGETHER + slot
                ahead = [table_ref[s * levels + level] > 0.0 for s in range(steps)]
                way = [jnp.where(a, 1, -1).astype(jnp.int32) for a in ahead]
                same = way[0] == way[1]
                first = jnp.where(same, cells - 9, cells - 6)
                inlet = [first - 6, jnp.int32(cells - 6)]
                base = [jnp.where(a, p, rows - 1 - p) for a, p in zip(ahead, inlet)]
                for r in range(6, rows - 6):
                    if r < cells:
                        at = pl.ds(pl.multiple_of((level * 18 + r - 6) * tracers, 8), tracers)
                        value = turned(chosen(True, near_ref[at, :], far_ref[at, :]), low_order)
                    elif r < 2 * cells:
                        value = own_ref[pl.ds(level * cells + r - cells, tracers, stride=levels * cells), :]
                    else:
                        at = pl.ds(pl.multiple_of((level * 18 + r - 2 * cells) * tracers, 8), tracers)
                        value = turned(chosen(False, near_ref[at, :], far_ref[at, :]), high_order)
                    q_a[slot, (r - base[0]) * way[0] + 6] = value
                flow.append((level, ahead, way, same, base))

            plan = [
                (0, 0, q_a, 3, q_b),
                (0, 1, q_b, 0, q_c),
                (0, 2, q_c, 0, q_d),
                (1, 0, q_d, 0, q_b),
                (1, 1, q_b, 0, q_c),
                (1, 2, q_c, 0, None),
            ]
            items = [(n, slot) for n in range(6) for slot in range(TOGETHER)]
            counts = [cells + 5 * (5 - n) for n in range(6)]
            parts = [-(-c // 2) for c in counts]
            pushed, popped = [0], [0]

            def push(item, part):
                n, slot = item
                _, _, source, pad, _ = plan[n]
                at = 2 * part + 3 + pad
                both = jnp.concatenate([source[slot, at], source[slot, at + 1]], axis=0)
                high = both.astype(jnp.bfloat16)
                rest = (both - high.astype(jnp.float32)).astype(jnp.bfloat16)
                lhs = jnp.concatenate([high, rest], axis=1)
                place = pushed[0] % SLOTS
                pushed[0] += 1
                for side in range(2):
                    pltpu.matmul_acc_lhs(accs[2 * place + side], lhs)

            state = {}

            def finish(item, part):
                n, slot = item
                s, number, source, pad, target = plan[n]
                level, ahead, way, same, base = flow[slot]
                weight = SECTION_WEIGHTS[number]
                place = popped[0] % SLOTS
                popped[0] += 1
                pops = [pltpu.matmul_pop(accs[2 * place + side]) for side in range(2)]
                if part == 0:
                    state.clear()

                def spot(k):
                    return base[s] + way[s] * (k + 3 * number)

                def spread(at, kind):
                    return jnp.broadcast_to(coef_ref[level, s, pl.ds(at * KINDS + kind, 1), :], (8, width))

                def q(k):
                    if k not in state:
                        state[k] = source[slot, k + pad]
                    return state[k]

                def along_x(k):
                    at = spot(k) + jnp.where(ahead[s], 0, 1)
                    five = ((q(k) - 6.5 * q(k + 1)) + (23.5 * q(k + 2) + 13.5 * q(k + 3))) - 1.5 * q(k + 4)
                    return spread(at, 0) * five

                if part == 0:
                    state["before"] = along_x(0)
                for half in range(2):
                    k = 2 * part + half
                    if k >= counts[n]:
                        continue
                    at = spot(k)
                    after = along_x(k + 1)
                    sides = []
                    for side in range(2):
                        flux = spread(at, 1 + side)
                        rows_of = pops[side][8 * half : 8 * half + 8]
                        sides.append(flux * jnp.where(flux >= 0.0, rows_of[:, :width], rows_of[:, width:]))
                    div = (after - state["before"]) + (sides[1] - sides[0])
                    if number == 0:
                        start = q(k + 3) * spread(at, 6)
                        start_ref[slot, k] = start
                    else:
                        start = start_ref[slot, k + 3 * number]
                    if weight != 1.0:
                        start = start * (1.0 / weight)
                    value = (start - div) * spread(at, 3 + number)
                    if target is None:
                        i = jnp.where(ahead[1], k, cells - 1 - k)
                        out_ref[pl.ds(level * cells + i, tracers, stride=levels * cells), :] = value
                    elif target is q_d:
                        q_d[slot, jnp.where(same, k, counts[n] - 1 - k)] = value
                    else:
                        target[slot, k] = value
                    state["before"] = after
                    state.pop(k, None)

            for part in range(parts[0]):
                push(items[0], part)
            for index, item in enumerate(items):
                following = items[index + 1] if index + 1 < len(items) else None
                ahead_parts = parts[following[0]] if following else 0
                for part in range(max(parts[item[0]], ahead_parts)):
                    if part < parts[item[0]]:
                        finish(item, part)
                    if part < ahead_parts:
                        push(following, part)
            return carry

        lax.fori_loop(0, levels // TOGETHER, group_body, 0)

    acc = [pltpu.ACC(side)((16, 256), jnp.float32) for _ in range(SLOTS) for side in range(2)]
    pl.run_scoped(run, *acc)


def edge_kernel(levels, cells, tracers, field_ref, table_ref, near_ref, far_ref):
    even = lax.rem(lax.axis_index("tile"), 2) == 0
    near_row = jnp.where(even, cells - 18, 0)
    far_row = cells - 18 - near_row

    def level_body(level, carry):
        for r in range(18):
            at = pl.ds(pl.multiple_of((level * 18 + r) * tracers, 8), tracers)
            for ref, row in ((near_ref, near_row), (far_ref, far_row)):
                ref[at, :] = field_ref[pl.ds(level * cells + row + r, tracers, stride=levels * cells), :]
        return carry

    lax.fori_loop(0, levels, level_body, 0)


def met_kernel(groups, steps, x_ref, y_ref, p_ref, out_ref):
    for s in range(steps):
        first = s * ROWS
        for ref in (x_ref, y_ref, p_ref):
            count = ref.shape[0] // steps
            value = ref[s * count : (s + 1) * count].reshape(count, ref.shape[2])
            for g in range(groups):
                out_ref[g, first : first + count, :] = value
            first += count


def block_kernel(met_ref, near_ref, far_ref):
    odd = lax.rem(lax.axis_index("tile"), 2) == 1

    def fill(above_ref, below_ref):
        for slot, (s, g) in enumerate([(0, g) for g in range(2, 8)] + [(1, 5), (1, 6), (1, 7)]):
            above_ref[slot * ROWS : (slot + 1) * ROWS, :] = met_ref[g, s * ROWS : (s + 1) * ROWS, :]
        for slot, (s, g) in enumerate([(1, 0), (1, 1), (1, 2)] + [(0, g) for g in range(6)]):
            below_ref[slot * ROWS : (slot + 1) * ROWS, :] = met_ref[g, s * ROWS : (s + 1) * ROWS, :]

    @pl.when(odd)
    def _():
        fill(far_ref, near_ref)

    @pl.when(jnp.logical_not(odd))
    def _():
        fill(near_ref, far_ref)


def local(tracers, wind_x, wind_y, surface_p, coef_a, coef_b, edge_flip):
    count, levels, cells, width = tracers.shape
    steps, block = wind_x.shape[0], wind_x.shape[3]
    groups, tiles = lax.axis_size("grp"), lax.axis_size("tile")
    stride = steps * ROWS
    smem = pl.BlockSpec(memory_space=pltpu.SMEM)
    vmem = pl.BlockSpec(memory_space=pltpu.VMEM)
    flat = (count * levels * cells, width)
    small = pltpu.CompilerParams(vmem_limit_bytes=8 * 1024 * 1024)
    edge = jax.ShapeDtypeStruct((levels * 18 * count, width), jnp.float32)

    near_pairs, far_pairs = pairs(tiles)
    table = jnp.concatenate(
        [wind_x[:, :, 0, 0, 0].reshape(-1), coef_a, coef_b, edge_flip.astype(jnp.float32)], axis=0
    )
    near, far = pl.pallas_call(
        functools.partial(edge_kernel, levels, cells, count),
        out_shape=(edge, edge),
        in_specs=[vmem, pl.BlockSpec(memory_space=pl.ANY)],
        out_specs=(vmem, vmem),
        compiler_params=small,
        name="edges",
    )(tracers.reshape(flat), table)
    near = lax.ppermute(near, "tile", near_pairs)
    far = lax.ppermute(far, "tile", far_pairs)
    packed = pl.pallas_call(
        functools.partial(met_kernel, groups, steps),
        out_shape=jax.ShapeDtypeStruct((groups, stride, width), jnp.float32),
        in_specs=[vmem] * 3,
        out_specs=vmem,
        name="met",
    )(wind_x.reshape(-1, 1, width), wind_y.reshape(-1, 1, width), surface_p.reshape(-1, 1, width))
    met = lax.all_to_all(packed, "grp", 0, 0, tiled=True)
    part = jax.ShapeDtypeStruct((9 * ROWS, width), jnp.float32)
    met_near, met_far = pl.pallas_call(
        block_kernel, out_shape=(part, part), in_specs=[vmem], out_specs=(vmem, vmem), compiler_params=small, name="blocks"
    )(met)
    met_near = lax.ppermute(met_near, "tile", near_pairs)
    met_far = lax.ppermute(met_far, "tile", far_pairs)

    met_flat = (groups * stride, width)
    dims = (steps, levels, cells, block, groups, count, stride)
    rows = 3 * cells
    out, mass = pl.pallas_call(
        functools.partial(advect_kernel, dims),
        out_shape=(
            jax.ShapeDtypeStruct(flat, jnp.float32),
            jax.ShapeDtypeStruct((levels * cells, width), jnp.float32),
        ),
        in_specs=[smem] + [vmem] * 6 + [pl.BlockSpec(memory_space=pltpu.HBM)],
        out_specs=(vmem, vmem),
        scratch_shapes=[
            pltpu.VMEM((TOGETHER, 64, count, width), jnp.float32),
            pltpu.VMEM((TOGETHER, 56, count, width), jnp.float32),
            pltpu.VMEM((TOGETHER, 56, count, width), jnp.float32),
            pltpu.VMEM((TOGETHER, 40, count, width), jnp.float32),
            pltpu.VMEM((TOGETHER, 56, count, width), jnp.float32),
            pltpu.VMEM((levels, steps, rows * KINDS, width), jnp.float32),
            pltpu.VMEM((2, 11 * ROWS, width), jnp.float32),
            pltpu.VMEM((2, 2 * width, 2 * width), jnp.bfloat16),
            pltpu.SemaphoreType.DMA,
        ],
        compiler_params=pltpu.CompilerParams(vmem_limit_bytes=VMEM_LIMIT),
        name="advect",
    )(
        table,
        tracers.reshape(flat),
        near,
        far,
        met.reshape(met_flat),
        met_near,
        met_far,
        jnp.asarray(stencil_weights(width)),
    )
    return out.reshape(tracers.shape), mass.reshape(levels, cells, width)


def solution(mesh):
    return jax.shard_map(
        local,
        mesh=mesh,
        in_specs=(
            P("grp", None, "tile", None),
            P(None, None, "tile", "grp", None),
            P(None, None, "tile", "grp", None),
            P(None, "tile", "grp", None),
            P(),
            P(),
            P(),
        ),
        out_specs=(P("grp", None, "tile", None), P(None, "tile", None)),
        check_vma=False,
    )
```

```python
import functools

import jax
import jax.numpy as jnp
import ml_dtypes
import numpy as np
from jax import lax
from jax.experimental import pallas as pl
from jax.experimental.pallas import tpu as pltpu
from jax.sharding import PartitionSpec as P

SECTION_WEIGHTS = (1.0 / 3.0, 0.5, 1.0)
TOGETHER = 3
ROWS = 64
KINDS = 6
SLOTS = 32
VMEM_LIMIT = 24 * 1024 * 1024


def pairs(count):
    near = [(i, i ^ 1) for i in range(count)]
    far = [(i, (i + (1 if i % 2 else -1)) % count) for i in range(count)]
    return near, far


def stencil_weights(width):
    out = np.zeros((2 * width, 2 * width), np.float32)
    for j in range(width):
        for tap, value in enumerate((2.0, -13.0, 47.0, 27.0, -3.0)):
            up = min(max(j - 3 + tap, 0), width - 1)
            down = min(max(j + 2 - tap, 0), width - 1)
            for half in (0, width):
                out[half + up, j] += value
                out[half + down, width + j] += value
    return out.astype(ml_dtypes.bfloat16)


def advect_kernel(
    dims,
    table_ref,
    own_ref,
    near_ref,
    far_ref,
    met_own_ref,
    met_near_ref,
    met_far_ref,
    weights_hbm,
    out_ref,
    mass_ref,
    q_a,
    q_b,
    q_c,
    q_d,
    start_ref,
    coef_ref,
    met_side_ref,
    weights_ref,
    weights_sem,
):
    steps, levels, cells, block, groups, tracers, stride = dims
    width = 128
    rows = 3 * cells
    tiles = lax.axis_size("tile")
    here = lax.axis_index("tile")
    gains = steps * levels
    flips = gains + 2 * levels
    low_flip = table_ref[flips + lax.rem(here + tiles - 1, tiles)]
    high_flip = table_ref[flips + here]
    odd = lax.rem(here, 2) == 1

    lane = lax.broadcasted_iota(jnp.int32, (8, width), 1)
    row = lax.broadcasted_iota(jnp.int32, (8, width), 0)
    first_row = row == 0
    last_row = row == groups - 1

    def order_of(flip):
        return jnp.where(flip == 1.0, width - 1 - lane, lane)

    def neighbour_orders(flip):
        flipped = flip == 1.0
        order = order_of(flip)
        before = jnp.where(flipped, jnp.minimum(order + 1, width - 1), jnp.maximum(order - 1, 0))
        after = jnp.where(flipped, jnp.maximum(order - 1, 0), jnp.minimum(order + 1, width - 1))
        return order, before, after

    low_orders = neighbour_orders(low_flip)
    high_orders = neighbour_orders(high_flip)
    low_order, high_order = low_orders[0], high_orders[0]
    low_sign = jnp.where(low_flip == 1.0, -1.0, 1.0).astype(jnp.float32)
    high_sign = jnp.where(high_flip == 1.0, -1.0, 1.0).astype(jnp.float32)

    odd_mask = jnp.where(odd, lane, lane - width) >= 0

    def chosen(below, near, far):
        return jnp.where(odd_mask, near, far) if below else jnp.where(odd_mask, far, near)

    def turned(values, order):
        return jnp.take_along_axis(values, order, axis=1)

    def shift(values, by):
        return pltpu.roll(values, by % width, 1)

    def coefficients(level, slot):
        gain_a = table_ref[gains + level]
        gain_b = table_ref[gains + levels + level]

        def take(t, s, first):
            if t == 1:
                return met_own_ref[pl.ds(s * ROWS + first, 8, stride=stride), :]
            return met_side_ref[t // 2, pl.ds((0 if (t == 0) == (s == 0) else 3) * ROWS + first, 8, stride=ROWS), :]

        orders = (low_orders, None, high_orders)
        signs = (low_sign, None, high_sign)
        mass = None
        for s in range(steps):
            flux_x = [[None] * block for _ in range(3)]
            faces_y = [[None] * block for _ in range(3)]
            start = [[None] * block for _ in range(3)]
            for t in range(3):
                for c in range(block):
                    at = level * block + c
                    pressure = take(t, s, 2 * levels * block + c)
                    met = gain_a + gain_b * pressure
                    x = take(t, s, at) * met
                    y = take(t, s, levels * block + at) * met
                    if orders[t] is not None:
                        order, order_before, order_after = orders[t]
                        x = turned(x, order)
                        y = y * signs[t]
                        y_before, y_after, y = turned(y, order_before), turned(y, order_after), turned(y, order)
                        if s == 0:
                            met = turned(met, order)
                    else:
                        y_before, y_after = shift(y, 1), shift(y, -1)
                    flux_x[t][c] = x
                    faces_y[t][c] = (
                        jnp.where(lane == 0, 0.0, 0.5 * (y_before + y)),
                        jnp.where(lane == width - 1, 0.0, 0.5 * (y + y_after)),
                    )
                    start[t][c] = met
            if s == 0:
                mass = start
            face_x = [[None] * block for _ in range(3)]
            for t in range(3):
                for c in range(block):
                    if c:
                        before = flux_x[t][c - 1]
                    else:
                        before = pltpu.roll(flux_x[t][block - 1], 1, 0)
                        if t:
                            before = jnp.where(first_row, pltpu.roll(flux_x[t - 1][block - 1], 1, 0), before)
                    face_x[t][c] = 0.5 * (before + flux_x[t][c])
            for t in range(3):
                for c in range(block):
                    if c < block - 1:
                        after = face_x[t][c + 1]
                    else:
                        after = pltpu.roll(face_x[t][0], groups - 1, 0)
                        if t < 2:
                            after = jnp.where(last_row, pltpu.roll(face_x[t + 1][0], groups - 1, 0), after)
                    face_y, next_y = faces_y[t][c]
                    div = (after - face_x[t][c]) + (next_y - face_y)
                    kinds = [jnp.abs(face_x[t][c]) * (1.0 / 30.0), face_y * (1.0 / 60.0)]
                    for weight in SECTION_WEIGHTS:
                        kinds.append(weight / (mass[t][c] - weight * div))
                    kinds.append(mass[t][c])
                    for kind, value in enumerate(kinds):
                        coef_ref[slot, s, pl.ds((t * cells + c) * KINDS + kind, 8, stride=KINDS * block), :] = value
                    mass[t][c] = mass[t][c] - div
        for c in range(block):
            mass_ref[pl.ds(level * cells + c, 8, stride=block), :] = mass[1][c]

    def run(*accs):
        fetch = pltpu.make_async_copy(weights_hbm, weights_ref, weights_sem)
        fetch.start()
        met_side_ref[0, 0 : 2 * ROWS, :] = jnp.zeros((2 * ROWS, width), jnp.float32)
        met_side_ref[1, 9 * ROWS : 11 * ROWS, :] = jnp.zeros((2 * ROWS, width), jnp.float32)
        for r in range(0, 9 * ROWS, 8):
            near, far = met_near_ref[r : r + 8, :], met_far_ref[r : r + 8, :]
            met_side_ref[0, 2 * ROWS + r : 2 * ROWS + r + 8, :] = chosen(True, near, far)
            met_side_ref[1, r : r + 8, :] = chosen(False, near, far)
        for level in range(levels):
            coefficients(level, level)

        fetch.wait()
        for side in range(2):
            pltpu.matmul_push_rhs(weights_ref[...], 0, side)
        for side in range(2):
            pltpu.matmul_acc_lhs(accs[side], jnp.zeros((16, 256), jnp.bfloat16), load_staged_rhs=0)
            out_ref[0:16, :] = pltpu.matmul_pop(accs[side])[:, :width]

        def group_body(group, carry):
            flow = []
            for slot in range(TOGETHER):
                level = group * TOGETHER + slot
                ahead = [table_ref[s * levels + level] > 0.0 for s in range(steps)]
                way = [jnp.where(a, 1, -1).astype(jnp.int32) for a in ahead]
                same = way[0] == way[1]
                first = jnp.where(same, cells - 9, cells - 6)
                inlet = [first - 6, jnp.int32(cells - 6)]
                base = [jnp.where(a, p, rows - 1 - p) for a, p in zip(ahead, inlet)]
                for r in range(6, rows - 6):
                    if r < cells:
                        at = pl.ds(pl.multiple_of((level * 18 + r - 6) * tracers, 8), tracers)
                        value = turned(chosen(True, near_ref[at, :], far_ref[at, :]), low_order)
                    elif r < 2 * cells:
                        value = own_ref[pl.ds(level * cells + r - cells, tracers, stride=levels * cells), :]
                    else:
                        at = pl.ds(pl.multiple_of((level * 18 + r - 2 * cells) * tracers, 8), tracers)
                        value = turned(chosen(False, near_ref[at, :], far_ref[at, :]), high_order)
                    q_a[slot, (r - base[0]) * way[0] + 6] = value
                flow.append((level, ahead, way, same, base))

            plan = [
                (0, 0, q_a, 3, q_b),
                (0, 1, q_b, 0, q_c),
                (0, 2, q_c, 0, q_d),
                (1, 0, q_d, 0, q_b),
                (1, 1, q_b, 0, q_c),
                (1, 2, q_c, 0, None),
            ]
            items = [(n, slot) for n in range(6) for slot in range(TOGETHER)]
            counts = [cells + 5 * (5 - n) for n in range(6)]
            parts = [-(-c // 2) for c in counts]
            pushed, popped = [0], [0]

            def push(item, part):
                n, slot = item
                _, _, source, pad, _ = plan[n]
                at = 2 * part + 3 + pad
                both = jnp.concatenate([source[slot, at], source[slot, at + 1]], axis=0)
                high = both.astype(jnp.bfloat16)
                rest = (both - high.astype(jnp.float32)).astype(jnp.bfloat16)
                lhs = jnp.concatenate([high, rest], axis=1)
                pltpu.matmul_acc_lhs(accs[pushed[0] % SLOTS], lhs)
                pushed[0] += 1

            state = {}

            def finish(item, part):
                n, slot = item
                s, number, source, pad, target = plan[n]
                level, ahead, way, same, base = flow[slot]
                weight = SECTION_WEIGHTS[number]
                pops = pltpu.matmul_pop(accs[popped[0] % SLOTS])
                popped[0] += 1
                if part == 0:
                    state.clear()

                def spot(k):
                    return base[s] + way[s] * (k + 3 * number)

                def spread(at, kind):
                    return jnp.broadcast_to(coef_ref[level, s, pl.ds(at * KINDS + kind, 1), :], (8, width))

                def q(k):
                    if k not in state:
                        state[k] = source[slot, k + pad]
                    return state[k]

                def along_x(k):
                    at = spot(k) + jnp.where(ahead[s], 0, 1)
                    five = ((q(k) - 6.5 * q(k + 1)) + (23.5 * q(k + 2) + 13.5 * q(k + 3))) - 1.5 * q(k + 4)
                    return spread(at, 0) * five

                if part == 0:
                    state["before"] = along_x(0)
                for half in range(2):
                    k = 2 * part + half
                    if k >= counts[n]:
                        continue
                    at = spot(k)
                    after = along_x(k + 1)
                    flux = spread(at, 1)
                    faces = pops[8 * half : 8 * half + 8]
                    along_y = flux * jnp.where(flux >= 0.0, faces[:, :width], faces[:, width:])
                    div = (after - state["before"]) + (shift(along_y, -1) - along_y)
                    if number == 0:
                        start = q(k + 3) * spread(at, 5)
                        start_ref[slot, k] = start
                    else:
                        start = start_ref[slot, k + 3 * number]
                    if weight != 1.0:
                        start = start * (1.0 / weight)
                    value = (start - div) * spread(at, 2 + number)
                    if target is None:
                        i = jnp.where(ahead[1], k, cells - 1 - k)
                        out_ref[pl.ds(level * cells + i, tracers, stride=levels * cells), :] = value
                    elif target is q_d:
                        q_d[slot, jnp.where(same, k, counts[n] - 1 - k)] = value
                    else:
                        target[slot, k] = value
                    state["before"] = after
                    state.pop(k, None)

            for part in range(parts[0]):
                push(items[0], part)
            for index, item in enumerate(items):
                following = items[index + 1] if index + 1 < len(items) else None
                ahead_parts = parts[following[0]] if following else 0
                for part in range(max(parts[item[0]], ahead_parts)):
                    if part < parts[item[0]]:
                        finish(item, part)
                    if part < ahead_parts:
                        push(following, part)
            return carry

        lax.fori_loop(0, levels // TOGETHER, group_body, 0)

    acc = [pltpu.ACC(place % 2)((16, 256), jnp.float32) for place in range(SLOTS)]
    pl.run_scoped(run, *acc)


def edge_kernel(levels, cells, tracers, field_ref, table_ref, near_ref, far_ref):
    even = lax.rem(lax.axis_index("tile"), 2) == 0
    near_row = jnp.where(even, cells - 18, 0)
    far_row = cells - 18 - near_row

    def level_body(level, carry):
        for r in range(18):
            at = pl.ds(pl.multiple_of((level * 18 + r) * tracers, 8), tracers)
            for ref, row in ((near_ref, near_row), (far_ref, far_row)):
                ref[at, :] = field_ref[pl.ds(level * cells + row + r, tracers, stride=levels * cells), :]
        return carry

    lax.fori_loop(0, levels, level_body, 0)


def met_kernel(groups, steps, x_ref, y_ref, p_ref, out_ref):
    for s in range(steps):
        first = s * ROWS
        for ref in (x_ref, y_ref, p_ref):
            count = ref.shape[0] // steps
            value = ref[s * count : (s + 1) * count].reshape(count, ref.shape[2])
            for g in range(groups):
                out_ref[g, first : first + count, :] = value
            first += count


def block_kernel(met_ref, near_ref, far_ref):
    odd = lax.rem(lax.axis_index("tile"), 2) == 1

    def fill(above_ref, below_ref):
        for slot, (s, g) in enumerate([(0, g) for g in range(2, 8)] + [(1, 5), (1, 6), (1, 7)]):
            above_ref[slot * ROWS : (slot + 1) * ROWS, :] = met_ref[g, s * ROWS : (s + 1) * ROWS, :]
        for slot, (s, g) in enumerate([(1, 0), (1, 1), (1, 2)] + [(0, g) for g in range(6)]):
            below_ref[slot * ROWS : (slot + 1) * ROWS, :] = met_ref[g, s * ROWS : (s + 1) * ROWS, :]

    @pl.when(odd)
    def _():
        fill(far_ref, near_ref)

    @pl.when(jnp.logical_not(odd))
    def _():
        fill(near_ref, far_ref)


def local(tracers, wind_x, wind_y, surface_p, coef_a, coef_b, edge_flip):
    count, levels, cells, width = tracers.shape
    steps, block = wind_x.shape[0], wind_x.shape[3]
    groups, tiles = lax.axis_size("grp"), lax.axis_size("tile")
    stride = steps * ROWS
    smem = pl.BlockSpec(memory_space=pltpu.SMEM)
    vmem = pl.BlockSpec(memory_space=pltpu.VMEM)
    flat = (count * levels * cells, width)
    small = pltpu.CompilerParams(vmem_limit_bytes=8 * 1024 * 1024)
    edge = jax.ShapeDtypeStruct((levels * 18 * count, width), jnp.float32)

    near_pairs, far_pairs = pairs(tiles)
    table = jnp.concatenate(
        [wind_x[:, :, 0, 0, 0].reshape(-1), coef_a, coef_b, edge_flip.astype(jnp.float32)], axis=0
    )
    near, far = pl.pallas_call(
        functools.partial(edge_kernel, levels, cells, count),
        out_shape=(edge, edge),
        in_specs=[vmem, pl.BlockSpec(memory_space=pl.ANY)],
        out_specs=(vmem, vmem),
        compiler_params=small,
        name="edges",
    )(tracers.reshape(flat), table)
    near = lax.ppermute(near, "tile", near_pairs)
    far = lax.ppermute(far, "tile", far_pairs)
    packed = pl.pallas_call(
        functools.partial(met_kernel, groups, steps),
        out_shape=jax.ShapeDtypeStruct((groups, stride, width), jnp.float32),
        in_specs=[vmem] * 3,
        out_specs=vmem,
        name="met",
    )(wind_x.reshape(-1, 1, width), wind_y.reshape(-1, 1, width), surface_p.reshape(-1, 1, width))
    met = lax.all_to_all(packed, "grp", 0, 0, tiled=True)
    part = jax.ShapeDtypeStruct((9 * ROWS, width), jnp.float32)
    met_near, met_far = pl.pallas_call(
        block_kernel, out_shape=(part, part), in_specs=[vmem], out_specs=(vmem, vmem), compiler_params=small, name="blocks"
    )(met)
    met_near = lax.ppermute(met_near, "tile", near_pairs)
    met_far = lax.ppermute(met_far, "tile", far_pairs)

    met_flat = (groups * stride, width)
    dims = (steps, levels, cells, block, groups, count, stride)
    rows = 3 * cells
    out, mass = pl.pallas_call(
        functools.partial(advect_kernel, dims),
        out_shape=(
            jax.ShapeDtypeStruct(flat, jnp.float32),
            jax.ShapeDtypeStruct((levels * cells, width), jnp.float32),
        ),
        in_specs=[smem] + [vmem] * 6 + [pl.BlockSpec(memory_space=pltpu.HBM)],
        out_specs=(vmem, vmem),
        scratch_shapes=[
            pltpu.VMEM((TOGETHER, 64, count, width), jnp.float32),
            pltpu.VMEM((TOGETHER, 56, count, width), jnp.float32),
            pltpu.VMEM((TOGETHER, 56, count, width), jnp.float32),
            pltpu.VMEM((TOGETHER, 40, count, width), jnp.float32),
            pltpu.VMEM((TOGETHER, 56, count, width), jnp.float32),
            pltpu.VMEM((levels, steps, rows * KINDS, width), jnp.float32),
            pltpu.VMEM((2, 11 * ROWS, width), jnp.float32),
            pltpu.VMEM((2 * width, 2 * width), jnp.bfloat16),
            pltpu.SemaphoreType.DMA,
        ],
        compiler_params=pltpu.CompilerParams(vmem_limit_bytes=VMEM_LIMIT),
        name="advect",
    )(
        table,
        tracers.reshape(flat),
        near,
        far,
        met.reshape(met_flat),
        met_near,
        met_far,
        jnp.asarray(stencil_weights(width)),
    )
    return out.reshape(tracers.shape), mass.reshape(levels, cells, width)


def solution(mesh):
    return jax.shard_map(
        local,
        mesh=mesh,
        in_specs=(
            P("grp", None, "tile", None),
            P(None, None, "tile", "grp", None),
            P(None, None, "tile", "grp", None),
            P(None, "tile", "grp", None),
            P(),
            P(),
            P(),
        ),
        out_specs=(P("grp", None, "tile", None), P(None, "tile", None)),
        check_vma=False,
    )
```
